32 devices in a mesh: energy: 8 (over z, y), tile: 4 (over x, core).
Axes of the slice: x: 2, y: 2, z: 4, core: 2. Of those that a mesh axis runs over, the one named last changes fastest.
Arguments:
- hamiltonian: float32 [256, 256], replicated, may hold values from -0.8 to 0.8
- onsite: float32 [32, 256], P(('energy', 'tile')), may hold values from 4 to 10
- inject: float32 [32, 256], P(('energy', 'tile')), may hold values from 5 to 50
- phonon_kernel: float32 [32, 32], replicated, may hold values from -1 to 1
- coupling: float32 [16, 9], replicated, may hold values from 0.3 to 1
- neighbours: int32 [16, 8], replicated, may hold values from 0 to 15, as said below
Outputs:
- sigma_blocks: float32 [32, 16, 9, 256], P(('energy', 'tile'))
- density: float32 [32, 256], P(('energy', 'tile'))
The draws below stay inside these ranges and needn't reach their ends.
Inputs may be any that keep to these rules, and one draw needn't show every extreme that they name: `neighbours`: row t lists 8 distinct tiles, none of them t.
All inputs are finite; a program needn't handle non-finite values.
Results may differ from the reference program's by a relative error of at most 0.0003.
Values sent between devices are 32-bit elements; how exact they have to be, the bound alone decides.
No kernel may reach another device: no remote copies, remote signals or barrier semaphores. Data moves between devices by JAX's collectives and lax.ppermute only.
A program may use at most 64 MiB of HBM per device.

```python
import math
import jax
import jax.numpy as jnp
from jax import lax

NORB = 256
B = 16
NBR = 8
SWEEPS = 3
ITERS = 2
NT = 16
NE = 32


def draw_neighbours(key, part):
    scores = jax.random.randint(key, (NT, NT), 0, 1 << 20, dtype=jnp.int32) * NT + jnp.arange(NT, dtype=jnp.int32)[None, :]
    itself = jnp.arange(NT, dtype=jnp.int32)[:, None] == jnp.arange(NT, dtype=jnp.int32)[None, :]
    scores = jnp.where(itself, -1, scores)
    values, chosen = lax.top_k(scores, NBR)
    return chosen.astype(jnp.int32)


def draw_hamiltonian(key, part):
    spread = 3.2 / math.sqrt(NORB)
    entries = jax.random.normal(key, (NORB, NORB), jnp.float32) * spread
    return jnp.clip(entries, -0.8, 0.8).astype(jnp.float32)


def shard_levels(key, shape, split, smallest, high):
    def one(position, shards_of):
        steps = jax.random.uniform(jax.random.fold_in(jax.random.fold_in(key, 6), position), (shards_of,), jnp.float32, smallest / len(split), high / len(split))
        return jnp.repeat(jnp.exp(steps), shape[position] // shards_of).reshape((-1,) + (1,) * (len(shape) - position - 1))

    gain = one(*split[0])
    for cut in split[1:]:
        gain = gain * one(*cut)
    return gain


def centred(key, dims, scale, bound, kind=jnp.bfloat16):
    values = jax.random.normal(key, dims, jnp.float32) * scale
    return jnp.minimum(jnp.maximum(values, -bound), bound).astype(kind)


def setup_inputs(seed: int = 0) -> dict:
    arg_keys = jax.random.split(jax.random.key(seed), 7)
    hamiltonian = draw_hamiltonian(jax.random.fold_in(arg_keys[6], 71), 0)
    onsite = jnp.clip(jnp.exp(math.log(10.0) - 0.916290732 * jax.random.uniform(arg_keys[1], (NE, NORB), jnp.float32) ** shard_levels(arg_keys[1], (NE, NORB), ((0, 32),), -0.2, 0.2)), 4.0, 10.0)
    inject = jnp.clip(jnp.exp(math.log(50.0) - 2.3025851 * jax.random.uniform(arg_keys[2], (NE, NORB), jnp.float32) ** shard_levels(arg_keys[2], (NE, NORB), ((0, 32),), -0.2, 0.2)), 5.0, 50.0)
    phonon_kernel = centred(arg_keys[3], (NE, NE), NE ** -0.5, 1.0, jnp.float32)
    coupling = jnp.clip(jax.random.uniform(arg_keys[4], (NT, NBR + 1), jnp.float32, 0.3, 1.0), 0.3, 1.0)
    neighbours = draw_neighbours(jax.random.fold_in(arg_keys[6], 71), 0)
    return {"hamiltonian": hamiltonian, "onsite": onsite, "inject": inject, "phonon_kernel": phonon_kernel, "coupling": coupling, "neighbours": neighbours}


highest = lax.Precision.HIGHEST


def tile_table(neighbours):
    listed = jnp.concatenate([jnp.arange(NT, dtype=jnp.int32)[:, None], neighbours.astype(jnp.int32)], axis=1)
    return (listed[:, :, None] == jnp.arange(NT, dtype=jnp.int32)[None, None, :]).astype(jnp.float32)


def extract(matrix, table):
    grid = matrix.reshape(NT, B, NT, B)
    picked = jnp.einsum('tjm,tamb->tjab', table, grid, precision=highest)
    return picked.reshape(NT, NBR + 1, B * B)


def assemble(blocks, table):
    blocks_four = blocks.reshape(NT, NBR + 1, B, B)
    grid = jnp.einsum('tjm,tjab->tamb', table, blocks_four, precision=highest)
    return grid.reshape(NORB, NORB)


def green(hamiltonian, table, sigma_flat, onsite_row, inject_row):
    sigma = assemble(sigma_flat, table)
    system = jnp.diag(onsite_row) - hamiltonian - sigma
    inverse = jnp.diag(1.0 / onsite_row)
    for repeat in range(SWEEPS):
        product = jnp.dot(inverse, system, precision=highest, preferred_element_type=jnp.float32)
        inverse = 2.0 * inverse - jnp.dot(product, inverse, precision=highest, preferred_element_type=jnp.float32)
    source = jnp.diag(inject_row) + sigma
    left = jnp.dot(inverse, source, precision=highest, preferred_element_type=jnp.float32)
    lesser = jnp.dot(left, inverse.T, precision=highest, preferred_element_type=jnp.float32)
    return extract(lesser, table), jnp.diagonal(lesser)


def reference(hamiltonian, onsite, inject, phonon_kernel, coupling, neighbours):
    table = tile_table(neighbours)
    sigma_blocks = jnp.zeros((NE, NT, NBR + 1, B * B), jnp.float32)
    density = jnp.zeros((NE, NORB), jnp.float32)

    def per_energy(items):
        return green(hamiltonian, table, items[0], items[1], items[2])

    for rounds in range(ITERS):
        lesser_blocks, density = lax.map(per_energy, (sigma_blocks, onsite, inject))
        mixed = jnp.dot(phonon_kernel, lesser_blocks.reshape(NE, -1), precision=highest, preferred_element_type=jnp.float32)
        sigma_blocks = mixed.reshape(NE, NT, NBR + 1, B * B) * coupling[None, :, :, None]
    return sigma_blocks, density
```

```python
import functools

import jax
import jax.numpy as jnp
from jax import lax
from jax.experimental import pallas as pl
from jax.experimental.pallas import tpu as pltpu
from jax.sharding import PartitionSpec as P

ITERS = 2
LANES = 128
UNROLL = 4

f32 = jnp.float32
VMEM = pl.BlockSpec(memory_space=pltpu.VMEM)
SMEM = pl.BlockSpec(memory_space=pltpu.SMEM)


def split(x):
    high = x.astype(jnp.bfloat16)
    return high, (x - high.astype(f32)).astype(jnp.bfloat16)


def dot3(a, b, dims=((1,), (0,))):
    def one(x, y):
        return lax.dot_general(x, y, (dims, ((), ())), preferred_element_type=f32)

    return one(a[0], b[0]) + (one(a[0], b[1]) + one(a[1], b[0]))


def series(n):
    n1 = split(n)
    square = dot3(n1, n1)
    n2 = split(square)
    cube = dot3(n2, n1)
    fourth = dot3(n2, n2)
    head = n + square + cube
    return head + fourth + dot3(split(fourth), split(head))


def eye(size):
    shape = (size, size)
    return lax.broadcasted_iota(jnp.int32, shape, 0) == lax.broadcasted_iota(jnp.int32, shape, 1)


def first_kernel(place, kernel_ref, levels_ref, h_ref, mine_ref, other_ref, columns):
    norb = h_ref.shape[0]
    half = levels_ref.shape[0] // 2
    me = place[0]
    start = lax.rem(me, 2) * half
    partner = me + 1 - 2 * lax.rem(me, 2)
    groups = columns.shape[0]
    unroll = half // groups
    for g in range(groups):
        rows = jnp.concatenate(
            [levels_ref[start + g * unroll + u, :, :norb] for u in range(unroll)], axis=0
        )
        rows = jnp.concatenate([rows] * (8 // unroll), axis=0) if unroll < 8 else rows
        columns[g, :, : rows.shape[0]] = (1.0 / rows).T
    mine_ref[...] = jnp.zeros_like(mine_ref)
    other_ref[...] = jnp.zeros_like(other_ref)
    diagonal = eye(norb)

    def group(g, carry):
        total_mine = jnp.zeros((norb, norb), f32)
        total_other = jnp.zeros((norb, norb), f32)
        for u in range(unroll):
            e = start + g * unroll + u
            row = levels_ref[e]
            n = h_ref[...] * (1.0 / row[:, :norb])
            s = series(n)
            green = jnp.where(diagonal, 1.0 + s, s) * columns[g, :, u : u + 1]
            lesser = dot3(split(green * row[:, norb:]), split(green), ((1,), (1,)))
            total_mine += kernel_ref[me, e] * lesser
            total_other += kernel_ref[partner, e] * lesser
        mine_ref[...] += total_mine
        other_ref[...] += total_other
        return carry

    lax.fori_loop(0, groups, group, 0)


def second_kernel(
    neighbours, coupling, mine_ref, other_ref, h_ref, onsite_ref, inject_ref, out_ref, density_ref,
    sigma, flat,
):
    norb = h_ref.shape[0]
    tiles, listed = coupling.shape
    b = norb // tiles
    lane_tile = lax.broadcasted_iota(jnp.int32, (1, norb), 1) // b
    for t in range(tiles):
        weight = jnp.where(lane_tile == t, coupling[t, 0], 0.0)
        for j in range(1, listed):
            weight = jnp.where(lane_tile == neighbours[t, j - 1], coupling[t, j], weight)
        rows = pl.ds(t * b, b)
        sigma[rows, :] = (mine_ref[rows, :] + other_ref[rows, :]) * weight
    diagonal = eye(norb)
    inverse_row = 1.0 / onsite_ref[...]
    inverse_column = jnp.broadcast_to(inverse_row, (8, norb)).T[:, :1]
    s = series((h_ref[...] + sigma[...]) * inverse_row)
    green = split(jnp.where(diagonal, 1.0 + s, s) * inverse_column)
    source = jnp.where(diagonal, sigma[...] + inject_ref[...], sigma[...])
    left = dot3(green, split(source))
    lesser = dot3(split(left), green, ((1,), (1,)))
    density_ref[...] = jnp.sum(jnp.where(diagonal, lesser, 0.0), axis=0, keepdims=True)
    sigma[...] = lesser
    flatten(sigma, flat, b)
    per = out_ref.shape[2] // LANES
    for t in range(tiles):
        for j in range(listed):
            m = t if j == 0 else neighbours[t, j - 1]
            for part in range(b * b // LANES):
                r = (t * listed + j) * (b * b // LANES) + part
                out_ref[r // per, :, pl.ds(r % per * LANES, LANES)] = flat[part, t * tiles + m]


def flatten(src, dst, b):
    per = LANES // b
    shape = (per, LANES)
    sub = lax.broadcasted_iota(jnp.int32, shape, 0)
    lane = lax.broadcasted_iota(jnp.int32, shape, 1)
    index = sub * b + lax.rem(lane, b)
    lane_group = lane // b
    norb = src.shape[0]
    for t in range(norb // b):
        for q in range(b // per):
            for h in range(norb // LANES):
                value = None
                for a in range(per):
                    row = src[pl.ds(t * b + q * per + a, 1), pl.ds(h * LANES, LANES)]
                    moved = jnp.take_along_axis(
                        jnp.broadcast_to(row, shape), index, axis=1, mode="promise_in_bounds"
                    )
                    value = moved if value is None else jnp.where(lane_group == a, moved, value)
                dst[q, pl.ds(t * b + h * per, per), 0, :] = value


def mix_kernel(kernel_ref, in_ref, out_ref):
    count = in_ref.shape[0]
    for k in range(in_ref.shape[2] // LANES):
        part = pl.ds(k * LANES, LANES)
        entries = in_ref[:, :, part].reshape(count, LANES)
        mixed = dot3(split(kernel_ref[...]), split(entries))
        out_ref[:, :, part] = mixed.reshape(count, 1, LANES)


def last_kernel(coupling, in_ref, out_ref):
    tiles, listed, size = out_ref.shape
    per = in_ref.shape[2] // LANES
    for t in range(tiles):
        for j in range(listed):
            for part in range(size // LANES):
                r = (t * listed + j) * (size // LANES) + part
                row = in_ref[r // per, :, pl.ds(r % per * LANES, LANES)]
                out_ref[t, pl.ds(j, 1), pl.ds(part * LANES, LANES)] = row * coupling[t, j]


def local(hamiltonian, onsite, inject, phonon_kernel, coupling, neighbours):
    axes = ("energy", "tile")
    tile_count = lax.axis_size("tile")
    count = lax.axis_size("energy") * tile_count
    norb = hamiltonian.shape[0]
    tiles, listed = coupling.shape
    size = (norb // tiles) ** 2
    me = lax.axis_index("energy") * tile_count + lax.axis_index("tile")

    levels = jnp.concatenate([onsite, inject], axis=1)
    levels = jnp.broadcast_to(levels[None], (count, 1, 2 * norb))
    levels = lax.all_to_all(levels, axes, split_axis=0, concat_axis=0, tiled=True)
    half = count // 2
    matrix = jax.ShapeDtypeStruct((norb, norb), f32)
    mine, other = pl.pallas_call(
        first_kernel,
        out_shape=(matrix, matrix),
        in_specs=[SMEM, SMEM, VMEM, VMEM],
        out_specs=(VMEM, VMEM),
        scratch_shapes=[pltpu.VMEM((half // UNROLL, norb, LANES), f32)],
    )(jnp.reshape(me, (1,)).astype(jnp.int32), phonon_kernel, levels, hamiltonian)
    pairs = [(i, i + 1 - 2 * (i % 2)) for i in range(tile_count)]
    other = lax.ppermute(other, "tile", pairs)

    per = -(-tiles * listed * size // (LANES * count))
    pieces = jax.ShapeDtypeStruct((count, 1, per * LANES), f32)
    rows, density = pl.pallas_call(
        second_kernel,
        out_shape=(pieces, jax.ShapeDtypeStruct((1, norb), f32)),
        in_specs=[SMEM, SMEM] + [VMEM] * 5,
        out_specs=(VMEM, VMEM),
        scratch_shapes=[
            pltpu.VMEM((norb, norb), f32),
            pltpu.VMEM((norb // LANES, norb, 1, LANES), f32),
        ],
    )(neighbours, coupling, mine, other, hamiltonian, onsite, inject)
    rows = lax.all_to_all(rows, axes, split_axis=0, concat_axis=0, tiled=True)
    rows = pl.pallas_call(
        mix_kernel, out_shape=pieces, in_specs=[VMEM] * 2, out_specs=VMEM
    )(phonon_kernel, rows)
    rows = lax.all_to_all(rows, axes, split_axis=0, concat_axis=0, tiled=True)
    sigma_blocks = pl.pallas_call(
        last_kernel,
        out_shape=jax.ShapeDtypeStruct((tiles, listed, size), f32),
        in_specs=[SMEM, VMEM],
        out_specs=VMEM,
    )(coupling, rows)
    return sigma_blocks[None], density


def solution(mesh):
    in_specs = (P(), P(("energy", "tile"), None), P(("energy", "tile"), None), P(), P(), P())
    out_specs = (P(("energy", "tile"), None, None, None), P(("energy", "tile"), None))
    return jax.shard_map(local, mesh=mesh, in_specs=in_specs, out_specs=out_specs, check_vma=False)
```

```python
import jax
import jax.numpy as jnp
from jax import lax
from jax.experimental import pallas as pl
from jax.experimental.pallas import tpu as pltpu
from jax.sharding import PartitionSpec as P

LANES = 128
UNROLL = 4

f32 = jnp.float32
VMEM = pl.BlockSpec(memory_space=pltpu.VMEM)
SMEM = pl.BlockSpec(memory_space=pltpu.SMEM)


def split(x):
    high = x.astype(jnp.bfloat16)
    return high, (x - high.astype(f32)).astype(jnp.bfloat16)


def dot(a, b, dims=((1,), (0,))):
    return lax.dot_general(a, b, (dims, ((), ())), preferred_element_type=f32)


def dot3(a, b, dims=((1,), (0,))):
    return dot(a[0], b[0], dims) + (dot(a[0], b[1], dims) + dot(a[1], b[0], dims))


def each(function, *lists):
    return [function(*items) for items in zip(*lists)]


def series(ns):
    first = each(split, ns)
    squares = each(dot3, first, first)
    second = each(split, squares)
    cubes = each(dot3, second, first)
    heads = each(lambda n, square, cube: n + square + cube, ns, squares, cubes)
    fourths = each(dot3, second, second)
    rests = each(dot3, each(split, fourths), each(split, heads))
    return each(lambda head, fourth, rest: head + fourth + rest, heads, fourths, rests)


def eye(size):
    shape = (size, size)
    return lax.broadcasted_iota(jnp.int32, shape, 0) == lax.broadcasted_iota(jnp.int32, shape, 1)


def call(kernel, out_shape, in_specs, scratch_shapes=(), vmem=8, flops=0):
    count = len(out_shape) if isinstance(out_shape, tuple) else 0
    return pl.pallas_call(
        kernel,
        out_shape=out_shape,
        in_specs=in_specs,
        out_specs=(VMEM,) * count if count else VMEM,
        scratch_shapes=scratch_shapes,
        compiler_params=pltpu.CompilerParams(vmem_limit_bytes=vmem << 20),
        cost_estimate=pl.CostEstimate(flops=flops, bytes_accessed=1 << 18, transcendentals=0),
    )


def levels_kernel(onsite_ref, inject_ref, out_ref):
    count, _, width = out_ref.shape
    norb = width // 2
    out_ref[:, :, :norb] = jnp.broadcast_to(onsite_ref[...].reshape(1, 1, norb), (count, 1, norb))
    out_ref[:, :, norb:] = jnp.broadcast_to(inject_ref[...].reshape(1, 1, norb), (count, 1, norb))


def tables_kernel(listed_t, coupling, weight_ref, lanes_ref):
    tiles, listed = coupling.shape
    norb = weight_ref.shape[0]
    b = norb // tiles
    group = lax.broadcasted_iota(jnp.int32, (b, norb), 1) // b
    slot = lax.broadcasted_iota(jnp.int32, (1, LANES), 1) // b
    for t in range(tiles):
        weight = jnp.where(group == t, coupling[t, 0], 0.0)
        tile = jnp.full((1, LANES), t, jnp.int32)
        for j in range(1, listed):
            m = listed_t[j - 1, t]
            weight = jnp.where(group == m, coupling[t, j], weight)
            tile = jnp.where(slot == j, m, tile)
        weight_ref[pl.ds(t * b, b), :] = weight
        lanes_ref[pl.ds(t, 1), :] = tile


def first_kernel(place, kernel_ref, levels_ref, h_ref, mine_ref, other_ref, columns):
    norb = h_ref.shape[0]
    half = levels_ref.shape[0] // 2
    me = place[0]
    start = lax.rem(me, 2) * half
    partner = me + 1 - 2 * lax.rem(me, 2)
    groups = columns.shape[0]
    unroll = half // groups
    for g in range(groups):
        rows = [levels_ref[start + g * unroll + u % unroll, :, :norb] for u in range(8)]
        columns[g, :, :8] = (1.0 / jnp.concatenate(rows, axis=0)).T
    mine_ref[...] = jnp.zeros_like(mine_ref)
    other_ref[...] = jnp.zeros_like(other_ref)
    diagonal = eye(norb)

    def group(g, carry):
        energies = [start + g * unroll + u for u in range(unroll)]
        rows = [levels_ref[e] for e in energies]
        sums = series([h_ref[...] * (1.0 / row[:, :norb]) for row in rows])
        total_mine = total_other = None
        for u in range(unroll):
            root = jnp.where(diagonal, 1.0 + sums[u], sums[u]) * columns[g, :, u : u + 1]
            high, low = split(root * jnp.sqrt(rows[u][:, norb:]))
            flip = ((1,), (1,))
            part = dot(high, high * jnp.bfloat16(0.5), flip) + dot(high, low, flip)
            mine = kernel_ref[me, energies[u]] * part
            other = kernel_ref[partner, energies[u]] * part
            total_mine = mine if u == 0 else total_mine + mine
            total_other = other if u == 0 else total_other + other
        mine_ref[...] += total_mine
        other_ref[...] += total_other
        return carry

    lax.fori_loop(0, groups, group, 0)


def lesser_function(weight_ref, mine_ref, other_ref, h_ref, onsite_ref, inject_ref):
    norb = h_ref.shape[0]
    total = mine_ref[...] + other_ref[...]
    sigma = (total + total.T) * weight_ref[...]
    diagonal = eye(norb)
    inverse_row = 1.0 / onsite_ref[...]
    inverse_column = jnp.broadcast_to(inverse_row, (8, norb)).T[:, :1]
    (s,) = series([(h_ref[...] + sigma) * inverse_row])
    green = split(jnp.where(diagonal, 1.0 + s, s) * inverse_column)
    source = jnp.where(diagonal, sigma + inject_ref[...], sigma)
    lesser = dot3(split(dot3(green, split(source))), green, ((1,), (1,)))
    return lesser, jnp.sum(jnp.where(diagonal, lesser, 0.0), axis=0, keepdims=True)


def second_kernel(
    listed_t, lanes_ref, weight_ref, mine_ref, other_ref, h_ref, onsite_ref, inject_ref,
    out_ref, density_ref, lesser_ref,
):
    lesser, density_ref[...] = lesser_function(
        weight_ref, mine_ref, other_ref, h_ref, onsite_ref, inject_ref
    )
    lesser_ref[...] = lesser
    norb = lesser_ref.shape[0]
    tiles = lanes_ref.shape[0]
    b = norb // tiles
    last = listed_t.shape[0]
    per = LANES // b
    shape = (per, LANES)
    lane = lax.broadcasted_iota(jnp.int32, shape, 1)
    own = lane // b == lax.broadcasted_iota(jnp.int32, shape, 0)

    def take(values, tile):
        index = lax.rem(tile, per) * b + lax.rem(lane, b)
        return jnp.take_along_axis(values, index, axis=1, mode="promise_in_bounds")

    for t in range(tiles):
        tile = jnp.broadcast_to(lanes_ref[pl.ds(t, 1), :], shape)
        m = listed_t[last - 1, t]
        for part in range(b // per):
            rows = pl.ds(t * b + part * per, per)
            value = take(lesser_ref[rows, :LANES], tile)
            for h in range(1, norb // LANES):
                columns = pl.ds(h * LANES, LANES)
                value = jnp.where(tile // per == h, take(lesser_ref[rows, columns], tile), value)
            columns = pl.ds(pl.multiple_of(m // per * LANES, LANES), LANES)
            block = take(lesser_ref[rows, columns], jnp.full(shape, m, jnp.int32))
            first = (t * (b // per) + part) * (per + 1)
            out_ref[pl.ds(first, per), :] = value
            out_ref[pl.ds(first + per, 1), :] = jnp.sum(
                jnp.where(own, block, 0.0), axis=0, keepdims=True
            )


def mix_kernel(kernel_ref, in_ref, out_ref):
    count = kernel_ref.shape[0]
    stride = in_ref.shape[0] // count
    kernel = split(kernel_ref[...])
    parts = [
        dot3(kernel, split(in_ref[pl.ds(k, count, stride=stride), :])) for k in range(stride)
    ]
    per = stride - 1
    width = LANES // per
    group = lax.broadcasted_iota(jnp.int32, (count, LANES), 1) // width
    step = 1
    while step < per:
        upper = (group // step) % 2 == 1
        for k in range(per):
            if k // step % 2 == 0:
                low, high = parts[k], parts[k + step]
                parts[k] = jnp.where(upper, pltpu.roll(high, step * width, 1), low)
                parts[k + step] = jnp.where(upper, high, pltpu.roll(low, LANES - step * width, 1))
        step *= 2
    for k in range(stride):
        out_ref[pl.ds(k, count, stride=stride), :] = parts[k]


def last_kernel(coupling_ref, in_ref, out_ref):
    listed, tiles, size = out_ref.shape
    parts = size // LANES
    for j in range(listed):
        weight = coupling_ref[:, j : j + 1]
        for part in range(parts):
            rows = in_ref[pl.ds(part * listed + j, tiles, stride=parts * listed), :]
            out_ref[j, :, pl.ds(part * LANES, LANES)] = rows * weight


def row_kernel(
    listed_t, weight_ref, mine_ref, other_ref, h_ref, onsite_ref, inject_ref,
    out_ref, density_ref, lesser_ref, flat,
):
    lesser, density_ref[...] = lesser_function(
        weight_ref, mine_ref, other_ref, h_ref, onsite_ref, inject_ref
    )
    lesser_ref[...] = lesser
    norb = lesser_ref.shape[0]
    listed = listed_t.shape[0] + 1
    tiles = listed_t.shape[1]
    b = norb // tiles
    flatten(lesser_ref, flat, b)
    per = out_ref.shape[2] // LANES
    parts = b * b // LANES
    for t in range(tiles):
        for j in range(listed):
            m = t if j == 0 else listed_t[j - 1, t]
            for part in range(parts):
                r = (t * listed + j) * parts + part
                out_ref[r // per, :, pl.ds(r % per * LANES, LANES)] = flat[part, t * tiles + m]


def flatten(src, dst, b):
    per = LANES // b
    shape = (per, LANES)
    lane = lax.broadcasted_iota(jnp.int32, shape, 1)
    index = lax.broadcasted_iota(jnp.int32, shape, 0) * b + lax.rem(lane, b)
    norb = src.shape[0]
    for t in range(norb // b):
        for q in range(b // per):
            for h in range(norb // LANES):
                value = None
                for a in range(per):
                    row = src[pl.ds(t * b + q * per + a, 1), pl.ds(h * LANES, LANES)]
                    moved = jnp.take_along_axis(
                        jnp.broadcast_to(row, shape), index, axis=1, mode="promise_in_bounds"
                    )
                    value = moved if value is None else jnp.where(lane // b == a, moved, value)
                dst[q, pl.ds(t * b + h * per, per), 0, :] = value


def row_mix_kernel(kernel_ref, in_ref, out_ref):
    count = in_ref.shape[0]
    kernel = split(kernel_ref[...])
    for k in range(in_ref.shape[2] // LANES):
        part = pl.ds(k * LANES, LANES)
        mixed = dot3(kernel, split(in_ref[:, :, part].reshape(count, LANES)))
        out_ref[:, :, part] = mixed.reshape(count, 1, LANES)


def row_last_kernel(coupling, in_ref, out_ref):
    listed, tiles, size = out_ref.shape
    per = in_ref.shape[2] // LANES
    for t in range(tiles):
        for j in range(listed):
            for part in range(size // LANES):
                r = (t * listed + j) * (size // LANES) + part
                row = in_ref[r // per, :, pl.ds(r % per * LANES, LANES)]
                out_ref[j, pl.ds(t, 1), pl.ds(part * LANES, LANES)] = row * coupling[t, j]


def local(hamiltonian, onsite, inject, phonon_kernel, coupling, neighbours):
    axes = ("energy", "tile")
    tile_count = lax.axis_size("tile")
    count = lax.axis_size("energy") * tile_count
    norb = hamiltonian.shape[0]
    tiles, listed = coupling.shape
    b = norb // tiles
    listed_t = neighbours.T

    def array(*shape, dtype=f32):
        return jax.ShapeDtypeStruct(shape, dtype)

    def exchange(x):
        return lax.all_to_all(x, axes, split_axis=0, concat_axis=0, tiled=True)

    levels = call(levels_kernel, array(count, 1, 2 * norb), [VMEM] * 2)(onsite, inject)
    levels = exchange(levels)
    weight, lanes = call(
        tables_kernel,
        (array(norb, norb), array(tiles, LANES, dtype=jnp.int32)),
        [SMEM] * 2,
    )(listed_t, coupling)

    me = lax.axis_index("energy") * tile_count + lax.axis_index("tile")
    half = count // 2
    mine, other = call(
        first_kernel,
        (array(norb, norb),) * 2,
        [SMEM, SMEM, VMEM, VMEM],
        [pltpu.VMEM((half // UNROLL, norb, LANES), f32)],
        vmem=24,
        flops=half * 14 * 2 * norb**3,
    )(jnp.reshape(me, (1,)).astype(jnp.int32), phonon_kernel, levels, hamiltonian)
    other = lax.ppermute(other, "tile", [(i, i + 1 - 2 * (i % 2)) for i in range(tile_count)])

    operands = (weight, mine, other, hamiltonian, onsite, inject)
    green_flops = 18 * 2 * norb**3
    dense = pltpu.VMEM((norb, norb), f32)
    if count * LANES == norb * b and listed * b == LANES + b:
        rows = array(norb * listed * b // LANES, LANES)
        pieces, density = call(
            second_kernel, (rows, array(1, norb)), [SMEM] + [VMEM] * 7, [dense], flops=green_flops
        )(listed_t, lanes, *operands)
        flat = (count, 1, rows.shape[0] * LANES // count)
        pieces = exchange(pieces.reshape(flat)).reshape(rows.shape)
        pieces = call(mix_kernel, rows, [VMEM] * 2)(phonon_kernel, pieces)
        pieces = exchange(pieces.reshape(flat)).reshape(rows.shape)
        blocks = call(last_kernel, array(listed, tiles, b * b), [VMEM] * 2)(coupling, pieces)
    else:
        per = -(-norb * listed * b // (LANES * count))
        rows = array(count, 1, per * LANES)
        pieces, density = call(
            row_kernel,
            (rows, array(1, norb)),
            [SMEM] + [VMEM] * 6,
            [dense, pltpu.VMEM((norb // LANES, norb, 1, LANES), f32)],
            flops=green_flops,
        )(listed_t, *operands)
        pieces = call(row_mix_kernel, rows, [VMEM] * 2)(phonon_kernel, exchange(pieces))
        blocks = call(row_last_kernel, array(listed, tiles, b * b), [SMEM, VMEM])(
            coupling, exchange(pieces)
        )
    return blocks.transpose(1, 0, 2)[None], density


def solution(mesh):
    in_specs = (P(), P(("energy", "tile"), None), P(("energy", "tile"), None), P(), P(), P())
    out_specs = (P(("energy", "tile"), None, None, None), P(("energy", "tile"), None))
    return jax.shard_map(local, mesh=mesh, in_specs=in_specs, out_specs=out_specs, check_vma=False)
```

```python
import jax
import jax.numpy as jnp
from jax import lax
from jax.experimental import pallas as pl
from jax.experimental.pallas import tpu as pltpu
from jax.sharding import PartitionSpec as P

LANES = 128
UNROLL = 5

f32 = jnp.float32
VMEM = pl.BlockSpec(memory_space=pltpu.VMEM)
SMEM = pl.BlockSpec(memory_space=pltpu.SMEM)
HBM = pl.BlockSpec(memory_space=pltpu.HBM)


def split(x):
    high = x.astype(jnp.bfloat16)
    return high, (x - high.astype(f32)).astype(jnp.bfloat16)


def dot(a, b, dims=((1,), (0,))):
    return lax.dot_general(a, b, (dims, ((), ())), preferred_element_type=f32)


def dot3(a, b, dims=((1,), (0,))):
    return dot(a[0], b[0], dims) + (dot(a[0], b[1], dims) + dot(a[1], b[0], dims))


def each(function, *lists):
    return [function(*items) for items in zip(*lists)]


def series(ns):
    first = each(split, ns)
    squares = each(dot3, first, first)
    second = each(split, squares)
    cubes = each(dot3, second, first)
    heads = each(lambda n, square, cube: n + square + cube, ns, squares, cubes)
    fourths = each(dot3, second, second)
    rests = each(dot3, each(split, fourths), each(split, heads))
    return each(lambda head, fourth, rest: head + fourth + rest, heads, fourths, rests)


def eye(size):
    shape = (size, size)
    return lax.broadcasted_iota(jnp.int32, shape, 0) == lax.broadcasted_iota(jnp.int32, shape, 1)


def call(kernel, out_shape, in_specs, scratch_shapes=(), vmem=8, flops=0):
    count = len(out_shape) if isinstance(out_shape, tuple) else 0
    return pl.pallas_call(
        kernel,
        out_shape=out_shape,
        in_specs=in_specs,
        out_specs=(VMEM,) * count if count else VMEM,
        scratch_shapes=scratch_shapes,
        compiler_params=pltpu.CompilerParams(vmem_limit_bytes=vmem << 20),
        cost_estimate=pl.CostEstimate(flops=flops, bytes_accessed=1 << 18, transcendentals=0),
    )


def levels_kernel(onsite_ref, inject_ref, out_ref, rows, sems):
    count, _, width = out_ref.shape
    norb = width // 2
    copies = [
        pltpu.make_async_copy(ref, rows.at[i], sems.at[i])
        for i, ref in enumerate((onsite_ref, inject_ref))
    ]
    for copy in copies:
        copy.start()
    for i, copy in enumerate(copies):
        copy.wait()
        out_ref[:, :, pl.ds(i * norb, norb)] = jnp.broadcast_to(rows[i][None], (count, 1, norb))


def weighted(h_ref, rows, columns, scales):
    norb = h_ref.shape[0]
    diagonal = eye(norb)
    sums = series([h_ref[...] * (1.0 / row[:, :norb]) for row in rows])
    totals = [None] * len(scales)
    for u, row in enumerate(rows):
        root = jnp.where(diagonal, 1.0 + sums[u], sums[u]) * columns[u]
        high, low = split(root * jnp.sqrt(row[:, norb:]))
        flip = ((1,), (1,))
        part = dot(high, high * jnp.bfloat16(0.5), flip) + dot(high, low, flip)
        for i, scale in enumerate(scales):
            totals[i] = scale[u] * part if u == 0 else totals[i] + scale[u] * part
    return totals


def own_kernel(
    place, listed_t, coupling, kernel_ref, h_ref, levels_ref,
    weight_ref, lanes_ref, mine_ref, other_ref,
):
    tiles, listed = coupling.shape
    norb = weight_ref.shape[0]
    b = norb // tiles
    row = levels_ref[0]
    column = jnp.broadcast_to(1.0 / row[:, :norb], (8, norb)).T[:, :1]
    me = place[0]
    partner = me + 1 - 2 * lax.rem(me, 2)
    scales = [[kernel_ref[target, me]] for target in (me, partner)]
    mine_ref[...], other_ref[...] = weighted(h_ref, [row], [column], scales)
    group = lax.broadcasted_iota(jnp.int32, (b, norb), 1) // b
    slot = lax.broadcasted_iota(jnp.int32, (1, LANES), 1) // b
    for t in range(tiles):
        weight = jnp.where(group == t, coupling[t, 0], 0.0)
        tile = jnp.full((1, LANES), t, jnp.int32)
        for j in range(1, listed):
            m = listed_t[j - 1, t]
            weight = jnp.where(group == m, coupling[t, j], weight)
            tile = jnp.where(slot == j, m, tile)
        weight_ref[pl.ds(t * b, b), :] = weight
        lanes_ref[pl.ds(t, 1), :] = tile


def first_kernel(
    place, kernel_ref, levels_ref, h_ref, own_mine_ref, own_other_ref,
    mine_ref, other_ref, columns,
):
    norb = h_ref.shape[0]
    half = levels_ref.shape[0] // 2
    me = place[0]
    parity = lax.rem(me, 2)
    partner = me + 1 - 2 * parity
    groups = columns.shape[0]
    unroll = -(-(half - 1) // groups)

    def energy(k):
        return 2 * lax.rem(me // 2 + jnp.minimum(k, half - 1), half) + parity

    def fill(g):
        rows = [levels_ref[energy(1 + g * unroll + u % unroll), :, :norb] for u in range(8)]
        columns[g, :, :8] = (1.0 / jnp.concatenate(rows, axis=0)).T

    for g in range(groups):
        fill(g)
    mine_ref[...] = own_mine_ref[...]
    other_ref[...] = own_other_ref[...]

    def group(g, carry):
        ks = [1 + g * unroll + u for u in range(unroll)]
        rows = [levels_ref[energy(k)] for k in ks]
        scales = [
            [jnp.where(k < half, kernel_ref[target, energy(k)], 0.0) for k in ks]
            for target in (me, partner)
        ]
        mine, other = weighted(
            h_ref, rows, [columns[g, :, u : u + 1] for u in range(unroll)], scales
        )
        mine_ref[...] += mine
        other_ref[...] += other
        return carry

    lax.fori_loop(0, groups, group, 0)


def lesser_function(place, weight_ref, mine_ref, other_ref, h_ref, levels_ref):
    norb = h_ref.shape[0]
    total = mine_ref[...] + other_ref[...]
    sigma = (total + total.T) * weight_ref[...]
    diagonal = eye(norb)
    row = levels_ref[place[0]]
    inverse_row = 1.0 / row[:, :norb]
    inverse_column = jnp.broadcast_to(inverse_row, (8, norb)).T[:, :1]
    (s,) = series([(h_ref[...] + sigma) * inverse_row])
    green = split(jnp.where(diagonal, 1.0 + s, s) * inverse_column)
    source = jnp.where(diagonal, sigma + row[:, norb:], sigma)
    lesser = dot3(split(dot3(green, split(source))), green, ((1,), (1,)))
    return lesser, jnp.sum(jnp.where(diagonal, lesser, 0.0), axis=0, keepdims=True)


def second_kernel(
    place, listed_t, lanes_ref, weight_ref, mine_ref, other_ref, h_ref, levels_ref,
    out_ref, density_ref, lesser_ref,
):
    lesser, density_ref[...] = lesser_function(
        place, weight_ref, mine_ref, other_ref, h_ref, levels_ref
    )
    lesser_ref[...] = lesser
    norb = lesser_ref.shape[0]
    tiles = lanes_ref.shape[0]
    b = norb // tiles
    last = listed_t.shape[0]
    per = LANES // b
    shape = (per, LANES)
    lane = lax.broadcasted_iota(jnp.int32, shape, 1)
    own = lane // b == lax.broadcasted_iota(jnp.int32, shape, 0)

    def take(values, tile):
        index = lax.rem(tile, per) * b + lax.rem(lane, b)
        return jnp.take_along_axis(values, index, axis=1, mode="promise_in_bounds")

    for t in range(tiles):
        tile = jnp.broadcast_to(lanes_ref[pl.ds(t, 1), :], shape)
        m = listed_t[last - 1, t]
        for part in range(b // per):
            rows = pl.ds(t * b + part * per, per)
            value = take(lesser_ref[rows, :LANES], tile)
            for h in range(1, norb // LANES):
                columns = pl.ds(h * LANES, LANES)
                value = jnp.where(tile // per == h, take(lesser_ref[rows, columns], tile), value)
            columns = pl.ds(pl.multiple_of(m // per * LANES, LANES), LANES)
            block = take(lesser_ref[rows, columns], jnp.full(shape, m, jnp.int32))
            first = (t * (b // per) + part) * (per + 1)
            out_ref[pl.ds(first, per), :] = value
            out_ref[pl.ds(first + per, 1), :] = jnp.sum(
                jnp.where(own, block, 0.0), axis=0, keepdims=True
            )


def mix_kernel(kernel_ref, in_ref, out_ref):
    count = kernel_ref.shape[0]
    stride = in_ref.shape[0] // count
    kernel = split(kernel_ref[...])
    parts = [
        dot3(kernel, split(in_ref[pl.ds(k, count, stride=stride), :])) for k in range(stride)
    ]
    per = stride - 1
    width = LANES // per
    group = lax.broadcasted_iota(jnp.int32, (count, LANES), 1) // width
    step = 1
    while step < per:
        upper = (group // step) % 2 == 1
        for k in range(per):
            if k // step % 2 == 0:
                low, high = parts[k], parts[k + step]
                parts[k] = jnp.where(upper, pltpu.roll(high, step * width, 1), low)
                parts[k + step] = jnp.where(upper, high, pltpu.roll(low, LANES - step * width, 1))
        step *= 2
    for k in range(stride):
        out_ref[pl.ds(k, count, stride=stride), :] = parts[k]


def last_kernel(coupling_ref, in_ref, diagonal_ref, out_ref, density_ref):
    density_ref[...] = diagonal_ref[...]
    listed, tiles, size = out_ref.shape
    parts = size // LANES
    for j in range(listed):
        weight = coupling_ref[:, j : j + 1]
        for part in range(parts):
            rows = in_ref[pl.ds(part * listed + j, tiles, stride=parts * listed), :]
            out_ref[j, :, pl.ds(part * LANES, LANES)] = rows * weight


def row_kernel(
    place, listed_t, weight_ref, mine_ref, other_ref, h_ref, levels_ref,
    out_ref, density_ref, lesser_ref, flat,
):
    lesser, density_ref[...] = lesser_function(
        place, weight_ref, mine_ref, other_ref, h_ref, levels_ref
    )
    lesser_ref[...] = lesser
    norb = lesser_ref.shape[0]
    listed = listed_t.shape[0] + 1
    tiles = listed_t.shape[1]
    b = norb // tiles
    flatten(lesser_ref, flat, b)
    per = out_ref.shape[2] // LANES
    parts = b * b // LANES
    for t in range(tiles):
        for j in range(listed):
            m = t if j == 0 else listed_t[j - 1, t]
            for part in range(parts):
                r = (t * listed + j) * parts + part
                out_ref[r // per, :, pl.ds(r % per * LANES, LANES)] = flat[part, t * tiles + m]


def flatten(src, dst, b):
    per = LANES // b
    shape = (per, LANES)
    lane = lax.broadcasted_iota(jnp.int32, shape, 1)
    index = lax.broadcasted_iota(jnp.int32, shape, 0) * b + lax.rem(lane, b)
    norb = src.shape[0]
    for t in range(norb // b):
        for q in range(b // per):
            for h in range(norb // LANES):
                value = None
                for a in range(per):
                    row = src[pl.ds(t * b + q * per + a, 1), pl.ds(h * LANES, LANES)]
                    moved = jnp.take_along_axis(
                        jnp.broadcast_to(row, shape), index, axis=1, mode="promise_in_bounds"
                    )
                    value = moved if value is None else jnp.where(lane // b == a, moved, value)
                dst[q, pl.ds(t * b + h * per, per), 0, :] = value


def row_mix_kernel(kernel_ref, in_ref, out_ref):
    count = in_ref.shape[0]
    kernel = split(kernel_ref[...])
    for k in range(in_ref.shape[2] // LANES):
        part = pl.ds(k * LANES, LANES)
        mixed = dot3(kernel, split(in_ref[:, :, part].reshape(count, LANES)))
        out_ref[:, :, part] = mixed.reshape(count, 1, LANES)


def row_last_kernel(coupling, in_ref, diagonal_ref, out_ref, density_ref):
    density_ref[...] = diagonal_ref[...]
    listed, tiles, size = out_ref.shape
    per = in_ref.shape[2] // LANES
    for t in range(tiles):
        for j in range(listed):
            for part in range(size // LANES):
                r = (t * listed + j) * (size // LANES) + part
                row = in_ref[r // per, :, pl.ds(r % per * LANES, LANES)]
                out_ref[j, pl.ds(t, 1), pl.ds(part * LANES, LANES)] = row * coupling[t, j]


def local(hamiltonian, onsite, inject, phonon_kernel, coupling, neighbours):
    axes = ("energy", "tile")
    tile_count = lax.axis_size("tile")
    count = lax.axis_size("energy") * tile_count
    norb = hamiltonian.shape[0]
    tiles, listed = coupling.shape
    b = norb // tiles
    listed_t = neighbours.T

    def array(*shape, dtype=f32):
        return jax.ShapeDtypeStruct(shape, dtype)

    def exchange(x):
        return lax.all_to_all(x, axes, split_axis=0, concat_axis=0, tiled=True)

    levels = call(
        levels_kernel,
        array(count, 1, 2 * norb),
        [HBM] * 2,
        [pltpu.VMEM((2, 1, norb), f32), pltpu.SemaphoreType.DMA((2,))],
        vmem=60,
    )(onsite, inject)
    all_levels = exchange(levels)
    me = lax.axis_index("energy") * tile_count + lax.axis_index("tile")
    place = jnp.reshape(me, (1,)).astype(jnp.int32)
    half = count // 2
    energy_flops = 14 * 2 * norb**3
    dense = array(norb, norb)
    weight, lanes, mine, other = call(
        own_kernel,
        (dense, array(tiles, LANES, dtype=jnp.int32), dense, dense),
        [SMEM] * 4 + [VMEM] * 2,
        flops=energy_flops,
    )(place, listed_t, coupling, phonon_kernel, hamiltonian, levels)
    mine, other = call(
        first_kernel,
        (dense, dense),
        [SMEM] * 2 + [VMEM] * 4,
        [pltpu.VMEM((-(-(half - 1) // UNROLL), norb, LANES), f32)],
        vmem=24,
        flops=(half - 1) * energy_flops,
    )(place, phonon_kernel, all_levels, hamiltonian, mine, other)
    other = lax.ppermute(other, "tile", [(i, i + 1 - 2 * (i % 2)) for i in range(tile_count)])

    operands = (weight, mine, other, hamiltonian, all_levels)
    green_flops = 18 * 2 * norb**3
    scratch = pltpu.VMEM((norb, norb), f32)
    results = (array(listed, tiles, b * b), array(1, norb))
    if count * LANES == norb * b and listed * b == LANES + b:
        rows = array(norb * listed * b // LANES, LANES)
        pieces, density = call(
            second_kernel,
            (rows, array(1, norb)),
            [SMEM] * 2 + [VMEM] * 6,
            [scratch],
            flops=green_flops,
        )(place, listed_t, lanes, *operands)
        flat = (count, 1, rows.shape[0] * LANES // count)
        pieces = exchange(pieces.reshape(flat)).reshape(rows.shape)
        pieces = call(mix_kernel, rows, [VMEM] * 2)(phonon_kernel, pieces)
        pieces = exchange(pieces.reshape(flat)).reshape(rows.shape)
        blocks, density = call(last_kernel, results, [VMEM] * 3)(coupling, pieces, density)
    else:
        per = -(-norb * listed * b // (LANES * count))
        rows = array(count, 1, per * LANES)
        pieces, density = call(
            row_kernel,
            (rows, array(1, norb)),
            [SMEM] * 2 + [VMEM] * 5,
            [scratch, pltpu.VMEM((norb // LANES, norb, 1, LANES), f32)],
            flops=green_flops,
        )(place, listed_t, *operands)
        pieces = call(row_mix_kernel, rows, [VMEM] * 2)(phonon_kernel, exchange(pieces))
        blocks, density = call(row_last_kernel, results, [SMEM, VMEM, VMEM])(
            coupling, exchange(pieces), density
        )
    return blocks.transpose(1, 0, 2)[None], density


def solution(mesh):
    in_specs = (P(), P(("energy", "tile"), None), P(("energy", "tile"), None), P(), P(), P())
    out_specs = (P(("energy", "tile"), None, None, None), P(("energy", "tile"), None))
    return jax.shard_map(local, mesh=mesh, in_specs=in_specs, out_specs=out_specs, check_vma=False)
```

```python
import jax
import jax.numpy as jnp
from jax import lax
from jax.experimental import pallas as pl
from jax.experimental.pallas import tpu as pltpu
from jax.sharding import PartitionSpec as P

LANES = 128
UNROLL = 5

f32 = jnp.float32
VMEM = pl.BlockSpec(memory_space=pltpu.VMEM)
SMEM = pl.BlockSpec(memory_space=pltpu.SMEM)
HBM = pl.BlockSpec(memory_space=pltpu.HBM)


def split(x):
    high = x.astype(jnp.bfloat16)
    return high, (x - high.astype(f32)).astype(jnp.bfloat16)


def dot(a, b, dims=((1,), (0,))):
    return lax.dot_general(a, b, (dims, ((), ())), preferred_element_type=f32)


def dot3(a, b, dims=((1,), (0,))):
    return dot(a[0], b[0], dims) + (dot(a[0], b[1], dims) + dot(a[1], b[0], dims))


def each(function, *lists):
    return [function(*items) for items in zip(*lists)]


def series(ns):
    first = each(split, ns)
    squares = each(dot3, first, first)
    second = each(split, squares)
    cubes = each(dot3, second, first)
    heads = each(lambda n, square, cube: n + square + cube, ns, squares, cubes)
    fourths = each(dot3, second, second)
    rests = each(dot3, each(split, fourths), each(split, heads))
    return each(lambda head, fourth, rest: head + fourth + rest, heads, fourths, rests)


def eye(size):
    shape = (size, size)
    return lax.broadcasted_iota(jnp.int32, shape, 0) == lax.broadcasted_iota(jnp.int32, shape, 1)


def call(kernel, out_shape, in_specs, scratch_shapes=(), vmem=8, flops=0):
    count = len(out_shape) if isinstance(out_shape, tuple) else 0
    return pl.pallas_call(
        kernel,
        out_shape=out_shape,
        in_specs=in_specs,
        out_specs=(VMEM,) * count if count else VMEM,
        scratch_shapes=scratch_shapes,
        compiler_params=pltpu.CompilerParams(vmem_limit_bytes=vmem << 20),
        cost_estimate=pl.CostEstimate(flops=flops, bytes_accessed=1 << 18, transcendentals=0),
    )


def position():
    me = lax.axis_index("energy") * lax.axis_size("tile") + lax.axis_index("tile")
    return me, me + 1 - 2 * lax.rem(me, 2)


def energy_of(k, half):
    me, _ = position()
    return 2 * lax.rem(me // 2 + jnp.minimum(k, half - 1), half) + lax.rem(me, 2)


def levels_kernel(onsite_ref, inject_ref, out_ref, rows, sems):
    count, _, width = out_ref.shape
    norb = width // 2
    copies = [
        pltpu.make_async_copy(ref, rows.at[i], sems.at[i])
        for i, ref in enumerate((onsite_ref, inject_ref))
    ]
    for copy in copies:
        copy.start()
    for i, copy in enumerate(copies):
        copy.wait()
        out_ref[:, :, pl.ds(i * norb, norb)] = jnp.broadcast_to(rows[i][None], (count, 1, norb))


def weighted(h_ref, rows, columns, scales):
    norb = h_ref.shape[0]
    diagonal = eye(norb)
    sums = series([h_ref[...] * (1.0 / row[:, :norb]) for row in rows])
    totals = [None] * len(scales)
    for u, row in enumerate(rows):
        root = jnp.where(diagonal, 1.0 + sums[u], sums[u]) * columns[u]
        high, low = split(root * jnp.sqrt(row[:, norb:]))
        flip = ((1,), (1,))
        part = dot(high, high * jnp.bfloat16(0.5), flip) + dot(high, low, flip)
        for i, scale in enumerate(scales):
            totals[i] = scale[u] * part if u == 0 else totals[i] + scale[u] * part
    return totals


def own_kernel(
    listed_t, coupling, kernel_ref, h_ref, levels_ref,
    weight_ref, lanes_ref, row_ref, scales_ref, mine_ref, other_ref,
):
    tiles, listed = coupling.shape
    norb = weight_ref.shape[0]
    b = norb // tiles
    row = levels_ref[0]
    row_ref[...] = row
    column = jnp.broadcast_to(1.0 / row[:, :norb], (8, norb)).T[:, :1]
    me, partner = position()
    scales = [[kernel_ref[target, me]] for target in (me, partner)]
    mine_ref[...], other_ref[...] = weighted(h_ref, [row], [column], scales)
    half = kernel_ref.shape[0] // 2
    for i, target in enumerate((me, partner)):
        for k in range(1, scales_ref.shape[1]):
            scale = kernel_ref[target, energy_of(k, half)] if k < half else 0.0
            scales_ref[i, k] = jnp.full((1, LANES), scale, f32)
    group = lax.broadcasted_iota(jnp.int32, (b, norb), 1) // b
    slot = lax.broadcasted_iota(jnp.int32, (1, LANES), 1) // b
    for t in range(tiles):
        weight = jnp.where(group == t, coupling[t, 0], 0.0)
        tile = jnp.full((1, LANES), t, jnp.int32)
        for j in range(1, listed):
            m = listed_t[j - 1, t]
            weight = jnp.where(group == m, coupling[t, j], weight)
            tile = jnp.where(slot == j, m, tile)
        weight_ref[pl.ds(t * b, b), :] = weight
        lanes_ref[pl.ds(t, 1), :LANES] = tile
        lanes_ref[pl.ds(t, 1), LANES:] = jnp.full((1, LANES), listed_t[listed - 2, t], jnp.int32)


def first_kernel(
    scales_ref, levels_ref, h_ref, own_mine_ref, own_other_ref, mine_ref, other_ref, columns
):
    norb = h_ref.shape[0]
    half = levels_ref.shape[0] // 2
    groups = columns.shape[0]
    unroll = (scales_ref.shape[1] - 1) // groups
    for g in range(groups):
        rows = [
            levels_ref[energy_of(1 + g * unroll + u % unroll, half), :, :norb] for u in range(8)
        ]
        columns[g, :, :8] = (1.0 / jnp.concatenate(rows, axis=0)).T
    mine_ref[...] = own_mine_ref[...]
    other_ref[...] = own_other_ref[...]

    def group(g, carry):
        ks = [1 + g * unroll + u for u in range(unroll)]
        rows = [levels_ref[energy_of(k, half)] for k in ks]
        scales = [
            [jnp.concatenate([scales_ref[i, k]] * (norb // LANES), axis=1) for k in ks]
            for i in range(2)
        ]
        mine, other = weighted(
            h_ref, rows, [columns[g, :, u : u + 1] for u in range(unroll)], scales
        )
        mine_ref[...] += mine
        other_ref[...] += other
        return carry

    lax.fori_loop(0, groups, group, 0)


def lesser_function(weight_ref, mine_ref, other_ref, h_ref, row_ref):
    norb = h_ref.shape[0]
    total = mine_ref[...] + other_ref[...]
    sigma = (total + total.T) * weight_ref[...]
    diagonal = eye(norb)
    row = row_ref[...]
    inverse_row = 1.0 / row[:, :norb]
    inverse_column = jnp.broadcast_to(inverse_row, (8, norb)).T[:, :1]
    (s,) = series([(h_ref[...] + sigma) * inverse_row])
    green = split(jnp.where(diagonal, 1.0 + s, s) * inverse_column)
    source = jnp.where(diagonal, sigma + row[:, norb:], sigma)
    lesser = dot3(split(dot3(green, split(source))), green, ((1,), (1,)))
    return lesser, jnp.sum(jnp.where(diagonal, lesser, 0.0), axis=0, keepdims=True)


def second_kernel(
    lanes_ref, weight_ref, mine_ref, other_ref, h_ref, row_ref,
    out_ref, density_ref, lesser_ref,
):
    lesser, density_ref[...] = lesser_function(
        weight_ref, mine_ref, other_ref, h_ref, row_ref
    )
    lesser_ref[...] = lesser
    norb = lesser_ref.shape[0]
    tiles = lanes_ref.shape[0]
    b = norb // tiles
    per = LANES // b
    shape = (per, LANES)
    lane = lax.broadcasted_iota(jnp.int32, shape, 1)
    own = lane // b == lax.broadcasted_iota(jnp.int32, shape, 0)

    def take(rows, tile):
        index = lax.rem(tile, per) * b + lax.rem(lane, b)
        value = None
        for h in range(norb // LANES):
            part = jnp.take_along_axis(
                lesser_ref[rows, pl.ds(h * LANES, LANES)], index, axis=1, mode="promise_in_bounds"
            )
            value = part if value is None else jnp.where(tile // per == h, part, value)
        return value

    for t in range(tiles):
        tile = jnp.broadcast_to(lanes_ref[pl.ds(t, 1), :LANES], shape)
        last = jnp.broadcast_to(lanes_ref[pl.ds(t, 1), LANES:], shape)
        for part in range(b // per):
            rows = pl.ds(t * b + part * per, per)
            first = (t * (b // per) + part) * (per + 1)
            out_ref[pl.ds(first, per), :] = take(rows, tile)
            out_ref[pl.ds(first + per, 1), :] = jnp.sum(
                jnp.where(own, take(rows, last), 0.0), axis=0, keepdims=True
            )


def mix_kernel(kernel_ref, in_ref, out_ref):
    count = kernel_ref.shape[0]
    stride = in_ref.shape[0] // count
    kernel = split(kernel_ref[...])
    parts = [
        dot3(kernel, split(in_ref[pl.ds(k, count, stride=stride), :])) for k in range(stride)
    ]
    per = stride - 1
    width = LANES // per
    group = lax.broadcasted_iota(jnp.int32, (count, LANES), 1) // width
    step = 1
    while step < per:
        upper = (group // step) % 2 == 1
        for k in range(per):
            if k // step % 2 == 0:
                low, high = parts[k], parts[k + step]
                parts[k] = jnp.where(upper, pltpu.roll(high, step * width, 1), low)
                parts[k + step] = jnp.where(upper, high, pltpu.roll(low, LANES - step * width, 1))
        step *= 2
    for k in range(stride):
        out_ref[pl.ds(k, count, stride=stride), :] = parts[k]


def last_kernel(coupling_ref, in_ref, diagonal_ref, out_ref, density_ref):
    density_ref[...] = diagonal_ref[...]
    listed, tiles, size = out_ref.shape
    parts = size // LANES
    for j in range(listed):
        weight = coupling_ref[:, j : j + 1]
        for part in range(parts):
            rows = in_ref[pl.ds(part * listed + j, tiles, stride=parts * listed), :]
            out_ref[j, :, pl.ds(part * LANES, LANES)] = rows * weight


def row_kernel(
    listed_t, weight_ref, mine_ref, other_ref, h_ref, row_ref,
    out_ref, density_ref, lesser_ref, flat,
):
    lesser, density_ref[...] = lesser_function(
        weight_ref, mine_ref, other_ref, h_ref, row_ref
    )
    lesser_ref[...] = lesser
    norb = lesser_ref.shape[0]
    listed = listed_t.shape[0] + 1
    tiles = listed_t.shape[1]
    b = norb // tiles
    flatten(lesser_ref, flat, b)
    per = out_ref.shape[2] // LANES
    parts = b * b // LANES
    for t in range(tiles):
        for j in range(listed):
            m = t if j == 0 else listed_t[j - 1, t]
            for part in range(parts):
                r = (t * listed + j) * parts + part
                out_ref[r // per, :, pl.ds(r % per * LANES, LANES)] = flat[part, t * tiles + m]


def flatten(src, dst, b):
    per = LANES // b
    shape = (per, LANES)
    lane = lax.broadcasted_iota(jnp.int32, shape, 1)
    index = lax.broadcasted_iota(jnp.int32, shape, 0) * b + lax.rem(lane, b)
    norb = src.shape[0]
    for t in range(norb // b):
        for q in range(b // per):
            for h in range(norb // LANES):
                value = None
                for a in range(per):
                    row = src[pl.ds(t * b + q * per + a, 1), pl.ds(h * LANES, LANES)]
                    moved = jnp.take_along_axis(
                        jnp.broadcast_to(row, shape), index, axis=1, mode="promise_in_bounds"
                    )
                    value = moved if value is None else jnp.where(lane // b == a, moved, value)
                dst[q, pl.ds(t * b + h * per, per), 0, :] = value


def row_mix_kernel(kernel_ref, in_ref, out_ref):
    count = in_ref.shape[0]
    kernel = split(kernel_ref[...])
    for k in range(in_ref.shape[2] // LANES):
        part = pl.ds(k * LANES, LANES)
        mixed = dot3(kernel, split(in_ref[:, :, part].reshape(count, LANES)))
        out_ref[:, :, part] = mixed.reshape(count, 1, LANES)


def row_last_kernel(coupling, in_ref, diagonal_ref, out_ref, density_ref):
    density_ref[...] = diagonal_ref[...]
    listed, tiles, size = out_ref.shape
    per = in_ref.shape[2] // LANES
    for t in range(tiles):
        for j in range(listed):
            for part in range(size // LANES):
                r = (t * listed + j) * (size // LANES) + part
                row = in_ref[r // per, :, pl.ds(r % per * LANES, LANES)]
                out_ref[j, pl.ds(t, 1), pl.ds(part * LANES, LANES)] = row * coupling[t, j]


def local(hamiltonian, onsite, inject, phonon_kernel, coupling, neighbours):
    axes = ("energy", "tile")
    tile_count = lax.axis_size("tile")
    count = lax.axis_size("energy") * tile_count
    norb = hamiltonian.shape[0]
    tiles, listed = coupling.shape
    b = norb // tiles
    listed_t = neighbours.T

    def array(*shape, dtype=f32):
        return jax.ShapeDtypeStruct(shape, dtype)

    def exchange(x):
        return lax.all_to_all(x, axes, split_axis=0, concat_axis=0, tiled=True)

    levels = call(
        levels_kernel,
        array(count, 1, 2 * norb),
        [HBM] * 2,
        [pltpu.VMEM((2, 1, norb), f32), pltpu.SemaphoreType.DMA((2,))],
        vmem=60,
    )(onsite, inject)
    all_levels = exchange(levels)
    half = count // 2
    groups = -(-(half - 1) // UNROLL)
    energy_flops = 14 * 2 * norb**3
    dense = array(norb, norb)
    scales = array(2, 1 + groups * UNROLL, 1, LANES)
    lanes = array(tiles, 2 * LANES, dtype=jnp.int32)
    weight, lanes, row, scales, mine, other = call(
        own_kernel,
        (dense, lanes, array(1, 2 * norb), scales, dense, dense),
        [SMEM] * 3 + [VMEM] * 2,
        flops=energy_flops,
    )(listed_t, coupling, phonon_kernel, hamiltonian, levels)
    mine, other = call(
        first_kernel,
        (dense, dense),
        [VMEM] * 5,
        [pltpu.VMEM((groups, norb, LANES), f32)],
        vmem=24,
        flops=(half - 1) * energy_flops,
    )(scales, all_levels, hamiltonian, mine, other)
    other = lax.ppermute(other, "tile", [(i, i + 1 - 2 * (i % 2)) for i in range(tile_count)])

    operands = (weight, mine, other, hamiltonian, row)
    green_flops = 18 * 2 * norb**3
    scratch = pltpu.VMEM((norb, norb), f32)
    results = (array(listed, tiles, b * b), array(1, norb))
    if count * LANES == norb * b and listed * b == LANES + b:
        rows = array(norb * listed * b // LANES, LANES)
        pieces, density = call(
            second_kernel,
            (rows, array(1, norb)),
            [VMEM] * 6,
            [scratch],
            flops=green_flops,
        )(lanes, *operands)
        flat = (count, 1, rows.shape[0] * LANES // count)
        pieces = exchange(pieces.reshape(flat)).reshape(rows.shape)
        pieces = call(mix_kernel, rows, [VMEM] * 2)(phonon_kernel, pieces)
        pieces = exchange(pieces.reshape(flat)).reshape(rows.shape)
        blocks, density = call(last_kernel, results, [VMEM] * 3)(coupling, pieces, density)
    else:
        per = -(-norb * listed * b // (LANES * count))
        rows = array(count, 1, per * LANES)
        pieces, density = call(
            row_kernel,
            (rows, array(1, norb)),
            [SMEM] + [VMEM] * 5,
            [scratch, pltpu.VMEM((norb // LANES, norb, 1, LANES), f32)],
            flops=green_flops,
        )(listed_t, *operands)
        pieces = call(row_mix_kernel, rows, [VMEM] * 2)(phonon_kernel, exchange(pieces))
        blocks, density = call(row_last_kernel, results, [SMEM, VMEM, VMEM])(
            coupling, exchange(pieces), density
        )
    return blocks.transpose(1, 0, 2)[None], density


def solution(mesh):
    in_specs = (P(), P(("energy", "tile"), None), P(("energy", "tile"), None), P(), P(), P())
    out_specs = (P(("energy", "tile"), None, None, None), P(("energy", "tile"), None))
    return jax.shard_map(local, mesh=mesh, in_specs=in_specs, out_specs=out_specs, check_vma=False)
```

```python
import jax
import jax.numpy as jnp
from jax import lax
from jax.experimental import pallas as pl
from jax.experimental.pallas import tpu as pltpu
from jax.sharding import PartitionSpec as P

LANES = 128
UNROLL = 5

f32 = jnp.float32
VMEM = pl.BlockSpec(memory_space=pltpu.VMEM)
SMEM = pl.BlockSpec(memory_space=pltpu.SMEM)


def split(x):
    high = x.astype(jnp.bfloat16)
    return high, (x - high.astype(f32)).astype(jnp.bfloat16)


def dot(a, b, dims=((1,), (0,))):
    return lax.dot_general(a, b, (dims, ((), ())), preferred_element_type=f32)


def dot3(a, b, dims=((1,), (0,))):
    return dot(a[0], b[0], dims) + (dot(a[0], b[1], dims) + dot(a[1], b[0], dims))


def each(function, *lists):
    return [function(*items) for items in zip(*lists)]


def series(ns):
    first = each(split, ns)
    squares = each(dot3, first, first)
    second = each(split, squares)
    cubes = each(dot3, second, first)
    heads = each(lambda n, square, cube: n + square + cube, ns, squares, cubes)
    fourths = each(dot3, second, second)
    rests = each(dot3, each(split, fourths), each(split, heads))
    return each(lambda head, fourth, rest: head + fourth + rest, heads, fourths, rests)


def eye(size):
    shape = (size, size)
    return lax.broadcasted_iota(jnp.int32, shape, 0) == lax.broadcasted_iota(jnp.int32, shape, 1)


def call(kernel, out_shape, in_specs, scratch_shapes=(), vmem=8, flops=0):
    count = len(out_shape) if isinstance(out_shape, tuple) else 0
    return pl.pallas_call(
        kernel,
        out_shape=out_shape,
        in_specs=in_specs,
        out_specs=(VMEM,) * count if count else VMEM,
        scratch_shapes=scratch_shapes,
        compiler_params=pltpu.CompilerParams(vmem_limit_bytes=vmem << 20),
        cost_estimate=pl.CostEstimate(flops=flops, bytes_accessed=1 << 18, transcendentals=0),
    )


def position():
    me = lax.axis_index("energy") * lax.axis_size("tile") + lax.axis_index("tile")
    return me, me + 1 - 2 * lax.rem(me, 2)


def energy_of(k, half):
    me, _ = position()
    return 2 * lax.rem(me // 2 + jnp.minimum(k, half - 1), half) + lax.rem(me, 2)


def weighted(h_ref, rows, columns, scales):
    norb = h_ref.shape[0]
    diagonal = eye(norb)
    sums = series([h_ref[...] * (1.0 / row[:1]) for row in rows])
    totals = [None] * len(scales)
    for u, row in enumerate(rows):
        root = jnp.where(diagonal, 1.0 + sums[u], sums[u]) * columns[u]
        high, low = split(root * jnp.sqrt(row[1:]))
        flip = ((1,), (1,))
        part = dot(high, high * jnp.bfloat16(0.5), flip) + dot(high, low, flip)
        for i, scale in enumerate(scales):
            totals[i] = scale[u] * part if u == 0 else totals[i] + scale[u] * part
    return totals


def own_kernel(
    listed_t, coupling, kernel_ref, h_ref, row_ref,
    weight_ref, lanes_ref, scales_ref, mine_ref, other_ref,
):
    tiles, listed = coupling.shape
    norb = weight_ref.shape[0]
    b = norb // tiles
    row = row_ref[...]
    column = jnp.broadcast_to(1.0 / row[:1], (8, norb)).T[:, :1]
    me, partner = position()
    scales = [[kernel_ref[target, me]] for target in (me, partner)]
    mine_ref[...], other_ref[...] = weighted(h_ref, [row], [column], scales)
    half = kernel_ref.shape[0] // 2
    for i, target in enumerate((me, partner)):
        for k in range(1, scales_ref.shape[1]):
            scale = kernel_ref[target, energy_of(k, half)] if k < half else 0.0
            scales_ref[i, k] = jnp.full((1, LANES), scale, f32)
    group = lax.broadcasted_iota(jnp.int32, (b, norb), 1) // b
    slot = lax.broadcasted_iota(jnp.int32, (1, LANES), 1) // b
    for t in range(tiles):
        weight = jnp.where(group == t, coupling[t, 0], 0.0)
        tile = jnp.full((1, LANES), t, jnp.int32)
        for j in range(1, listed):
            m = listed_t[j - 1, t]
            weight = jnp.where(group == m, coupling[t, j], weight)
            tile = jnp.where(slot == j, m, tile)
        weight_ref[pl.ds(t * b, b), :] = weight
        lanes_ref[pl.ds(t, 1), :LANES] = tile
        lanes_ref[pl.ds(t, 1), LANES:] = jnp.full((1, LANES), listed_t[listed - 2, t], jnp.int32)


def first_kernel(
    scales_ref, levels_ref, h_ref, own_mine_ref, own_other_ref, mine_ref, other_ref, columns
):
    norb = h_ref.shape[0]
    half = levels_ref.shape[0] // 2
    groups = columns.shape[0]
    unroll = (scales_ref.shape[1] - 1) // groups
    for g in range(groups):
        rows = [
            levels_ref[energy_of(1 + g * unroll + u % unroll, half), :1] for u in range(8)
        ]
        columns[g, :, :8] = (1.0 / jnp.concatenate(rows, axis=0)).T
    mine_ref[...] = own_mine_ref[...]
    other_ref[...] = own_other_ref[...]

    def group(g, carry):
        ks = [1 + g * unroll + u for u in range(unroll)]
        rows = [levels_ref[energy_of(k, half)] for k in ks]
        scales = [
            [jnp.concatenate([scales_ref[i, k]] * (norb // LANES), axis=1) for k in ks]
            for i in range(2)
        ]
        mine, other = weighted(
            h_ref, rows, [columns[g, :, u : u + 1] for u in range(unroll)], scales
        )
        mine_ref[...] += mine
        other_ref[...] += other
        return carry

    lax.fori_loop(0, groups, group, 0)


def lesser_function(weight_ref, mine_ref, other_ref, h_ref, row_ref):
    norb = h_ref.shape[0]
    total = mine_ref[...] + other_ref[...]
    sigma = (total + total.T) * weight_ref[...]
    diagonal = eye(norb)
    row = row_ref[...]
    inverse_row = 1.0 / row[:1]
    inverse_column = jnp.broadcast_to(inverse_row, (8, norb)).T[:, :1]
    (s,) = series([(h_ref[...] + sigma) * inverse_row])
    green = split(jnp.where(diagonal, 1.0 + s, s) * inverse_column)
    source = jnp.where(diagonal, sigma + row[1:], sigma)
    lesser = dot3(split(dot3(green, split(source))), green, ((1,), (1,)))
    return lesser, jnp.sum(jnp.where(diagonal, lesser, 0.0), axis=0, keepdims=True)


def second_kernel(
    lanes_ref, weight_ref, mine_ref, other_ref, h_ref, row_ref,
    out_ref, density_ref, lesser_ref,
):
    lesser, density_ref[...] = lesser_function(
        weight_ref, mine_ref, other_ref, h_ref, row_ref
    )
    lesser_ref[...] = lesser
    norb = lesser_ref.shape[0]
    tiles = lanes_ref.shape[0]
    b = norb // tiles
    per = LANES // b
    shape = (per, LANES)
    lane = lax.broadcasted_iota(jnp.int32, shape, 1)
    own = lane // b == lax.broadcasted_iota(jnp.int32, shape, 0)

    def take(rows, tile):
        index = lax.rem(tile, per) * b + lax.rem(lane, b)
        value = None
        for h in range(norb // LANES):
            part = jnp.take_along_axis(
                lesser_ref[rows, pl.ds(h * LANES, LANES)], index, axis=1, mode="promise_in_bounds"
            )
            value = part if value is None else jnp.where(tile // per == h, part, value)
        return value

    for t in range(tiles):
        tile = jnp.broadcast_to(lanes_ref[pl.ds(t, 1), :LANES], shape)
        last = jnp.broadcast_to(lanes_ref[pl.ds(t, 1), LANES:], shape)
        for part in range(b // per):
            rows = pl.ds(t * b + part * per, per)
            first = (t * (b // per) + part) * (per + 1)
            out_ref[pl.ds(first, per), :] = take(rows, tile)
            out_ref[pl.ds(first + per, 1), :] = jnp.sum(
                jnp.where(own, take(rows, last), 0.0), axis=0, keepdims=True
            )


def mix_kernel(kernel_ref, in_ref, out_ref):
    count = kernel_ref.shape[0]
    stride = in_ref.shape[0] // count
    kernel = split(kernel_ref[...])
    parts = [
        dot3(kernel, split(in_ref[pl.ds(k, count, stride=stride), :])) for k in range(stride)
    ]
    per = stride - 1
    width = LANES // per
    group = lax.broadcasted_iota(jnp.int32, (count, LANES), 1) // width
    step = 1
    while step < per:
        upper = (group // step) % 2 == 1
        for k in range(per):
            if k // step % 2 == 0:
                low, high = parts[k], parts[k + step]
                parts[k] = jnp.where(upper, pltpu.roll(high, step * width, 1), low)
                parts[k + step] = jnp.where(upper, high, pltpu.roll(low, LANES - step * width, 1))
        step *= 2
    for k in range(stride):
        out_ref[pl.ds(k, count, stride=stride), :] = parts[k]


def last_kernel(coupling_ref, in_ref, diagonal_ref, out_ref, density_ref):
    density_ref[...] = diagonal_ref[...]
    listed, tiles, size = out_ref.shape
    parts = size // LANES
    for j in range(listed):
        weight = coupling_ref[:, j : j + 1]
        for part in range(parts):
            rows = in_ref[pl.ds(part * listed + j, tiles, stride=parts * listed), :]
            out_ref[j, :, pl.ds(part * LANES, LANES)] = rows * weight


def row_kernel(
    listed_t, weight_ref, mine_ref, other_ref, h_ref, row_ref,
    out_ref, density_ref, lesser_ref, flat,
):
    lesser, density_ref[...] = lesser_function(
        weight_ref, mine_ref, other_ref, h_ref, row_ref
    )
    lesser_ref[...] = lesser
    norb = lesser_ref.shape[0]
    listed = listed_t.shape[0] + 1
    tiles = listed_t.shape[1]
    b = norb // tiles
    flatten(lesser_ref, flat, b)
    per = out_ref.shape[2] // LANES
    parts = b * b // LANES
    for t in range(tiles):
        for j in range(listed):
            m = t if j == 0 else listed_t[j - 1, t]
            for part in range(parts):
                r = (t * listed + j) * parts + part
                out_ref[r // per, :, pl.ds(r % per * LANES, LANES)] = flat[part, t * tiles + m]


def flatten(src, dst, b):
    per = LANES // b
    shape = (per, LANES)
    lane = lax.broadcasted_iota(jnp.int32, shape, 1)
    index = lax.broadcasted_iota(jnp.int32, shape, 0) * b + lax.rem(lane, b)
    norb = src.shape[0]
    for t in range(norb // b):
        for q in range(b // per):
            for h in range(norb // LANES):
                value = None
                for a in range(per):
                    row = src[pl.ds(t * b + q * per + a, 1), pl.ds(h * LANES, LANES)]
                    moved = jnp.take_along_axis(
                        jnp.broadcast_to(row, shape), index, axis=1, mode="promise_in_bounds"
                    )
                    value = moved if value is None else jnp.where(lane // b == a, moved, value)
                dst[q, pl.ds(t * b + h * per, per), 0, :] = value


def row_mix_kernel(kernel_ref, in_ref, out_ref):
    count = in_ref.shape[0]
    kernel = split(kernel_ref[...])
    for k in range(in_ref.shape[2] // LANES):
        part = pl.ds(k * LANES, LANES)
        mixed = dot3(kernel, split(in_ref[:, :, part].reshape(count, LANES)))
        out_ref[:, :, part] = mixed.reshape(count, 1, LANES)


def row_last_kernel(coupling, in_ref, diagonal_ref, out_ref, density_ref):
    density_ref[...] = diagonal_ref[...]
    listed, tiles, size = out_ref.shape
    per = in_ref.shape[2] // LANES
    for t in range(tiles):
        for j in range(listed):
            for part in range(size // LANES):
                r = (t * listed + j) * (size // LANES) + part
                row = in_ref[r // per, :, pl.ds(r % per * LANES, LANES)]
                out_ref[j, pl.ds(t, 1), pl.ds(part * LANES, LANES)] = row * coupling[t, j]


def local(hamiltonian, onsite, inject, phonon_kernel, coupling, neighbours):
    axes = ("energy", "tile")
    tile_count = lax.axis_size("tile")
    count = lax.axis_size("energy") * tile_count
    norb = hamiltonian.shape[0]
    tiles, listed = coupling.shape
    b = norb // tiles
    listed_t = neighbours.T

    def array(*shape, dtype=f32):
        return jax.ShapeDtypeStruct(shape, dtype)

    def exchange(x):
        return lax.all_to_all(x, axes, split_axis=0, concat_axis=0, tiled=True)

    row = jnp.stack([onsite, inject], axis=1).reshape(2, norb)
    all_levels = exchange(jnp.broadcast_to(row[None], (count, 2, norb)))
    half = count // 2
    groups = -(-(half - 1) // UNROLL)
    energy_flops = 14 * 2 * norb**3
    dense = array(norb, norb)
    scales = array(2, 1 + groups * UNROLL, 1, LANES)
    lanes = array(tiles, 2 * LANES, dtype=jnp.int32)
    weight, lanes, scales, mine, other = call(
        own_kernel,
        (dense, lanes, scales, dense, dense),
        [SMEM] * 3 + [VMEM] * 2,
        flops=energy_flops,
    )(listed_t, coupling, phonon_kernel, hamiltonian, row)
    mine, other = call(
        first_kernel,
        (dense, dense),
        [VMEM] * 5,
        [pltpu.VMEM((groups, norb, LANES), f32)],
        vmem=24,
        flops=(half - 1) * energy_flops,
    )(scales, all_levels, hamiltonian, mine, other)
    other = lax.ppermute(other, "tile", [(i, i + 1 - 2 * (i % 2)) for i in range(tile_count)])

    operands = (weight, mine, other, hamiltonian, row)
    green_flops = 18 * 2 * norb**3
    scratch = pltpu.VMEM((norb, norb), f32)
    results = (array(listed, tiles, b * b), array(1, norb))
    if count * LANES == norb * b and listed * b == LANES + b:
        rows = array(norb * listed * b // LANES, LANES)
        pieces, density = call(
            second_kernel,
            (rows, array(1, norb)),
            [VMEM] * 6,
            [scratch],
            flops=green_flops,
        )(lanes, *operands)
        flat = (count, 1, rows.shape[0] * LANES // count)
        pieces = exchange(pieces.reshape(flat)).reshape(rows.shape)
        pieces = call(mix_kernel, rows, [VMEM] * 2)(phonon_kernel, pieces)
        pieces = exchange(pieces.reshape(flat)).reshape(rows.shape)
        blocks, density = call(last_kernel, results, [VMEM] * 3)(coupling, pieces, density)
    else:
        per = -(-norb * listed * b // (LANES * count))
        rows = array(count, 1, per * LANES)
        pieces, density = call(
            row_kernel,
            (rows, array(1, norb)),
            [SMEM] + [VMEM] * 5,
            [scratch, pltpu.VMEM((norb // LANES, norb, 1, LANES), f32)],
            flops=green_flops,
        )(listed_t, *operands)
        pieces = call(row_mix_kernel, rows, [VMEM] * 2)(phonon_kernel, exchange(pieces))
        blocks, density = call(row_last_kernel, results, [SMEM, VMEM, VMEM])(
            coupling, exchange(pieces), density
        )
    return blocks.transpose(1, 0, 2)[None], density


def solution(mesh):
    in_specs = (P(), P(("energy", "tile"), None), P(("energy", "tile"), None), P(), P(), P())
    out_specs = (P(("energy", "tile"), None, None, None), P(("energy", "tile"), None))
    return jax.shard_map(local, mesh=mesh, in_specs=in_specs, out_specs=out_specs, check_vma=False)
```

```python
import jax
import jax.numpy as jnp
from jax import lax
from jax.experimental import pallas as pl
from jax.experimental.pallas import tpu as pltpu
from jax.sharding import PartitionSpec as P

LANES = 128
UNROLL = 15

f32 = jnp.float32
VMEM = pl.BlockSpec(memory_space=pltpu.VMEM)
SMEM = pl.BlockSpec(memory_space=pltpu.SMEM)


def split(x):
    high = x.astype(jnp.bfloat16)
    return high, (x - high.astype(f32)).astype(jnp.bfloat16)


def dot(a, b, dims=((1,), (0,))):
    return lax.dot_general(a, b, (dims, ((), ())), preferred_element_type=f32)


def dot3(a, b, dims=((1,), (0,))):
    return dot(a[0], b[0], dims) + (dot(a[0], b[1], dims) + dot(a[1], b[0], dims))


SHARE = 64.0 / 65.0


def blend(x):
    high = x.astype(jnp.bfloat16)
    low = (x - high.astype(f32)).astype(jnp.bfloat16)
    return high, low * jnp.bfloat16(8.125) + high * jnp.bfloat16(0.125)


def dot2(a, b):
    return dot(a[0], b[0]) + dot(a[1], b[1])


def each(function, *lists):
    return [function(*items) for items in zip(*lists)]


def series(ns):
    first = each(split, ns)
    squares = each(dot3, first, first)
    second = each(split, squares)
    cubes = each(dot3, second, first)
    heads = each(lambda n, square, cube: n + square + cube, ns, squares, cubes)
    fourths = each(dot3, second, second)
    rests = each(dot3, each(split, fourths), each(split, heads))
    return each(lambda head, fourth, rest: head + fourth + rest, heads, fourths, rests)


def eye(size):
    shape = (size, size)
    return lax.broadcasted_iota(jnp.int32, shape, 0) == lax.broadcasted_iota(jnp.int32, shape, 1)


def call(kernel, out_shape, in_specs, scratch_shapes=(), vmem=8, flops=0):
    count = len(out_shape) if isinstance(out_shape, tuple) else 0
    return pl.pallas_call(
        kernel,
        out_shape=out_shape,
        in_specs=in_specs,
        out_specs=(VMEM,) * count if count else VMEM,
        scratch_shapes=scratch_shapes,
        compiler_params=pltpu.CompilerParams(vmem_limit_bytes=vmem << 20),
        cost_estimate=pl.CostEstimate(flops=flops, bytes_accessed=1 << 18, transcendentals=0),
    )


def position():
    me = lax.axis_index("energy") * lax.axis_size("tile") + lax.axis_index("tile")
    return me, me + 1 - 2 * lax.rem(me, 2)


def energy_of(k, half):
    me, _ = position()
    return 2 * lax.rem(me // 2 + jnp.minimum(k, half - 1), half) + lax.rem(me, 2)


def weighted(h_ref, rows, columns, scales, targets):
    diagonal = eye(h_ref.shape[0])

    def one(row, column, factors):
        n = h_ref[...] * (SHARE / row[:1])
        first = split(n)
        square = dot3(first, first) * (1.0 / SHARE)
        yield
        first, second = blend(n), blend(square)
        cube = dot2(second, first)
        fourth = dot2(second, second)
        yield
        head = n + square + cube
        rest = dot2(blend(fourth), blend(head))
        yield
        s = head + fourth + rest
        root = jnp.where(diagonal, SHARE + s, s) * column
        high, low = split(root * (jnp.sqrt(row[1:]) / SHARE))
        flip = ((1,), (1,))
        part = dot(high, high * jnp.bfloat16(0.5), flip) + dot(high, low, flip)
        yield
        for factor, target in zip(factors, targets):
            target[...] += factor * part

    waiting = [one(row, columns[u], scales[u]) for u, row in enumerate(rows)]
    running = []
    while waiting or running:
        running += waiting[:1]
        waiting = waiting[1:]
        for stages in list(running):
            if next(stages, 0) == 0:
                running.remove(stages)


def own_kernel(
    listed_t, coupling, kernel_ref, h_ref, row_ref,
    weight_ref, lanes_ref, scales_ref, mine_ref, other_ref,
):
    tiles, listed = coupling.shape
    norb = weight_ref.shape[0]
    b = norb // tiles
    row = row_ref[...]
    column = jnp.broadcast_to(1.0 / row[:1], (8, norb)).T[:, :1]
    me, partner = position()
    mine_ref[...] = jnp.zeros_like(mine_ref)
    other_ref[...] = jnp.zeros_like(other_ref)
    scales = [kernel_ref[target, me] for target in (me, partner)]
    weighted(h_ref, [row], [column], [scales], (mine_ref, other_ref))
    half = kernel_ref.shape[0] // 2
    for i, target in enumerate((me, partner)):
        for k in range(1, scales_ref.shape[1]):
            scale = kernel_ref[target, energy_of(k, half)] if k < half else 0.0
            scales_ref[i, k] = jnp.full((1, LANES), scale, f32)
    group = lax.broadcasted_iota(jnp.int32, (b, norb), 1) // b
    slot = lax.broadcasted_iota(jnp.int32, (1, LANES), 1) // b
    for t in range(tiles):
        weight = jnp.where(group == t, coupling[t, 0], 0.0)
        tile = jnp.full((1, LANES), t, jnp.int32)
        for j in range(1, listed):
            m = listed_t[j - 1, t]
            weight = jnp.where(group == m, coupling[t, j], weight)
            tile = jnp.where(slot == j, m, tile)
        weight_ref[pl.ds(t * b, b), :] = weight
        lanes_ref[pl.ds(t, 1), :LANES] = tile
        lanes_ref[pl.ds(t, 1), LANES:] = jnp.full((1, LANES), listed_t[listed - 2, t], jnp.int32)


def first_kernel(
    scales_ref, levels_ref, h_ref, own_mine_ref, own_other_ref, mine_ref, other_ref, columns
):
    norb = h_ref.shape[0]
    half = levels_ref.shape[0] // 2
    groups = columns.shape[0]
    unroll = (scales_ref.shape[1] - 1) // groups
    for g in range(groups):
        rows = [levels_ref[energy_of(1 + g * unroll + u, half), :1] for u in range(unroll)]
        rows += rows[:1] * (-unroll % 8)
        columns[g, :, : len(rows)] = (1.0 / jnp.concatenate(rows, axis=0)).T
    mine_ref[...] = own_mine_ref[...]
    other_ref[...] = own_other_ref[...]

    def group(g, carry):
        ks = [1 + g * unroll + u for u in range(unroll)]
        rows = [levels_ref[energy_of(k, half)] for k in ks]
        scales = [
            [jnp.concatenate([scales_ref[i, k]] * (norb // LANES), axis=1) for i in range(2)]
            for k in ks
        ]
        weighted(
            h_ref, rows, [columns[g, :, u : u + 1] for u in range(unroll)], scales,
            (mine_ref, other_ref),
        )
        return carry

    lax.fori_loop(0, groups, group, 0)


def lesser_function(weight_ref, mine_ref, other_ref, h_ref, row_ref):
    norb = h_ref.shape[0]
    total = mine_ref[...] + other_ref[...]
    sigma = (total + total.T) * weight_ref[...]
    diagonal = eye(norb)
    row = row_ref[...]
    inverse_row = 1.0 / row[:1]
    inverse_column = jnp.broadcast_to(inverse_row, (8, norb)).T[:, :1]
    (s,) = series([(h_ref[...] + sigma) * inverse_row])
    green = split(jnp.where(diagonal, 1.0 + s, s) * inverse_column)
    source = jnp.where(diagonal, sigma + row[1:], sigma)
    lesser = dot3(split(dot3(green, split(source))), green, ((1,), (1,)))
    return lesser, jnp.sum(jnp.where(diagonal, lesser, 0.0), axis=0, keepdims=True)


def second_kernel(
    lanes_ref, weight_ref, mine_ref, other_ref, h_ref, row_ref,
    out_ref, density_ref, lesser_ref,
):
    lesser, density_ref[...] = lesser_function(
        weight_ref, mine_ref, other_ref, h_ref, row_ref
    )
    lesser_ref[...] = lesser
    norb = lesser_ref.shape[0]
    tiles = lanes_ref.shape[0]
    b = norb // tiles
    per = LANES // b
    shape = (per, LANES)
    lane = lax.broadcasted_iota(jnp.int32, shape, 1)
    own = lane // b == lax.broadcasted_iota(jnp.int32, shape, 0)

    def take(rows, tile):
        index = lax.rem(tile, per) * b + lax.rem(lane, b)
        value = None
        for h in range(norb // LANES):
            part = jnp.take_along_axis(
                lesser_ref[rows, pl.ds(h * LANES, LANES)], index, axis=1, mode="promise_in_bounds"
            )
            value = part if value is None else jnp.where(tile // per == h, part, value)
        return value

    for t in range(tiles):
        tile = jnp.broadcast_to(lanes_ref[pl.ds(t, 1), :LANES], shape)
        last = jnp.broadcast_to(lanes_ref[pl.ds(t, 1), LANES:], shape)
        for part in range(b // per):
            rows = pl.ds(t * b + part * per, per)
            first = (t * (b // per) + part) * (per + 1)
            out_ref[pl.ds(first, per), :] = take(rows, tile)
            out_ref[pl.ds(first + per, 1), :] = jnp.sum(
                jnp.where(own, take(rows, last), 0.0), axis=0, keepdims=True
            )


def mix_kernel(kernel_ref, in_ref, out_ref):
    count = kernel_ref.shape[0]
    stride = in_ref.shape[0] // count
    kernel = split(kernel_ref[...])
    parts = [
        dot3(kernel, split(in_ref[pl.ds(k, count, stride=stride), :])) for k in range(stride)
    ]
    per = stride - 1
    width = LANES // per
    group = lax.broadcasted_iota(jnp.int32, (count, LANES), 1) // width
    step = 1
    while step < per:
        upper = (group // step) % 2 == 1
        for k in range(per):
            if k // step % 2 == 0:
                low, high = parts[k], parts[k + step]
                parts[k] = jnp.where(upper, pltpu.roll(high, step * width, 1), low)
                parts[k + step] = jnp.where(upper, high, pltpu.roll(low, LANES - step * width, 1))
        step *= 2
    for k in range(stride):
        out_ref[pl.ds(k, count, stride=stride), :] = parts[k]


def last_kernel(coupling_ref, in_ref, diagonal_ref, out_ref, density_ref):
    density_ref[...] = diagonal_ref[...]
    listed, tiles, size = out_ref.shape
    parts = size // LANES
    for j in range(listed):
        weight = coupling_ref[:, j : j + 1]
        for part in range(parts):
            rows = in_ref[pl.ds(part * listed + j, tiles, stride=parts * listed), :]
            out_ref[j, :, pl.ds(part * LANES, LANES)] = rows * weight


def row_kernel(
    listed_t, weight_ref, mine_ref, other_ref, h_ref, row_ref,
    out_ref, density_ref, lesser_ref, flat,
):
    lesser, density_ref[...] = lesser_function(
        weight_ref, mine_ref, other_ref, h_ref, row_ref
    )
    lesser_ref[...] = lesser
    norb = lesser_ref.shape[0]
    listed = listed_t.shape[0] + 1
    tiles = listed_t.shape[1]
    b = norb // tiles
    flatten(lesser_ref, flat, b)
    per = out_ref.shape[2] // LANES
    parts = b * b // LANES
    for t in range(tiles):
        for j in range(listed):
            m = t if j == 0 else listed_t[j - 1, t]
            for part in range(parts):
                r = (t * listed + j) * parts + part
                out_ref[r // per, :, pl.ds(r % per * LANES, LANES)] = flat[part, t * tiles + m]


def flatten(src, dst, b):
    per = LANES // b
    shape = (per, LANES)
    lane = lax.broadcasted_iota(jnp.int32, shape, 1)
    index = lax.broadcasted_iota(jnp.int32, shape, 0) * b + lax.rem(lane, b)
    norb = src.shape[0]
    for t in range(norb // b):
        for q in range(b // per):
            for h in range(norb // LANES):
                value = None
                for a in range(per):
                    row = src[pl.ds(t * b + q * per + a, 1), pl.ds(h * LANES, LANES)]
                    moved = jnp.take_along_axis(
                        jnp.broadcast_to(row, shape), index, axis=1, mode="promise_in_bounds"
                    )
                    value = moved if value is None else jnp.where(lane // b == a, moved, value)
                dst[q, pl.ds(t * b + h * per, per), 0, :] = value


def row_mix_kernel(kernel_ref, in_ref, out_ref):
    count = in_ref.shape[0]
    kernel = split(kernel_ref[...])
    for k in range(in_ref.shape[2] // LANES):
        part = pl.ds(k * LANES, LANES)
        mixed = dot3(kernel, split(in_ref[:, :, part].reshape(count, LANES)))
        out_ref[:, :, part] = mixed.reshape(count, 1, LANES)


def row_last_kernel(coupling, in_ref, diagonal_ref, out_ref, density_ref):
    density_ref[...] = diagonal_ref[...]
    listed, tiles, size = out_ref.shape
    per = in_ref.shape[2] // LANES
    for t in range(tiles):
        for j in range(listed):
            for part in range(size // LANES):
                r = (t * listed + j) * (size // LANES) + part
                row = in_ref[r // per, :, pl.ds(r % per * LANES, LANES)]
                out_ref[j, pl.ds(t, 1), pl.ds(part * LANES, LANES)] = row * coupling[t, j]


def local(hamiltonian, onsite, inject, phonon_kernel, coupling, neighbours):
    axes = ("energy", "tile")
    tile_count = lax.axis_size("tile")
    count = lax.axis_size("energy") * tile_count
    norb = hamiltonian.shape[0]
    tiles, listed = coupling.shape
    b = norb // tiles
    listed_t = neighbours.T

    def array(*shape, dtype=f32):
        return jax.ShapeDtypeStruct(shape, dtype)

    def exchange(x):
        return lax.all_to_all(x, axes, split_axis=0, concat_axis=0, tiled=True)

    row = jnp.stack([onsite, inject], axis=1).reshape(2, norb)
    all_levels = exchange(jnp.broadcast_to(row[None], (count, 2, norb)))
    half = count // 2
    groups = -(-(half - 1) // UNROLL)
    energy_flops = 14 * 2 * norb**3
    dense = array(norb, norb)
    scales = array(2, 1 + groups * UNROLL, 1, LANES)
    lanes = array(tiles, 2 * LANES, dtype=jnp.int32)
    weight, lanes, scales, mine, other = call(
        own_kernel,
        (dense, lanes, scales, dense, dense),
        [SMEM] * 3 + [VMEM] * 2,
        flops=energy_flops,
    )(listed_t, coupling, phonon_kernel, hamiltonian, row)
    mine, other = call(
        first_kernel,
        (dense, dense),
        [VMEM] * 5,
        [pltpu.VMEM((groups, norb, LANES), f32)],
        vmem=24,
        flops=(half - 1) * energy_flops,
    )(scales, all_levels, hamiltonian, mine, other)
    other = lax.ppermute(other, "tile", [(i, i + 1 - 2 * (i % 2)) for i in range(tile_count)])

    operands = (weight, mine, other, hamiltonian, row)
    green_flops = 18 * 2 * norb**3
    scratch = pltpu.VMEM((norb, norb), f32)
    results = (array(listed, tiles, b * b), array(1, norb))
    if count * LANES == norb * b and listed * b == LANES + b:
        rows = array(norb * listed * b // LANES, LANES)
        pieces, density = call(
            second_kernel,
            (rows, array(1, norb)),
            [VMEM] * 6,
            [scratch],
            flops=green_flops,
        )(lanes, *operands)
        flat = (count, 1, rows.shape[0] * LANES // count)
        pieces = exchange(pieces.reshape(flat)).reshape(rows.shape)
        pieces = call(mix_kernel, rows, [VMEM] * 2)(phonon_kernel, pieces)
        pieces = exchange(pieces.reshape(flat)).reshape(rows.shape)
        blocks, density = call(last_kernel, results, [VMEM] * 3)(coupling, pieces, density)
    else:
        per = -(-norb * listed * b // (LANES * count))
        rows = array(count, 1, per * LANES)
        pieces, density = call(
            row_kernel,
            (rows, array(1, norb)),
            [SMEM] + [VMEM] * 5,
            [scratch, pltpu.VMEM((norb // LANES, norb, 1, LANES), f32)],
            flops=green_flops,
        )(listed_t, *operands)
        pieces = call(row_mix_kernel, rows, [VMEM] * 2)(phonon_kernel, exchange(pieces))
        blocks, density = call(row_last_kernel, results, [SMEM, VMEM, VMEM])(
            coupling, exchange(pieces), density
        )
    return blocks.transpose(1, 0, 2)[None], density


def solution(mesh):
    in_specs = (P(), P(("energy", "tile"), None), P(("energy", "tile"), None), P(), P(), P())
    out_specs = (P(("energy", "tile"), None, None, None), P(("energy", "tile"), None))
    return jax.shard_map(local, mesh=mesh, in_specs=in_specs, out_specs=out_specs, check_vma=False)
```

```python
import jax
import jax.numpy as jnp
from jax import lax
from jax.experimental import pallas as pl
from jax.experimental.pallas import tpu as pltpu
from jax.sharding import PartitionSpec as P

LANES = 128
UNROLL = 15

f32 = jnp.float32
VMEM = pl.BlockSpec(memory_space=pltpu.VMEM)
SMEM = pl.BlockSpec(memory_space=pltpu.SMEM)


def split(x):
    high = x.astype(jnp.bfloat16)
    return high, (x - high.astype(f32)).astype(jnp.bfloat16)


def dot(a, b, dims=((1,), (0,))):
    return lax.dot_general(a, b, (dims, ((), ())), preferred_element_type=f32)


def dot3(a, b, dims=((1,), (0,))):
    return dot(a[0], b[0], dims) + (dot(a[0], b[1], dims) + dot(a[1], b[0], dims))


SHARE = 64.0 / 65.0


def blend(x):
    high = x.astype(jnp.bfloat16)
    low = (x - high.astype(f32)).astype(jnp.bfloat16)
    return high, low * jnp.bfloat16(8.125) + high * jnp.bfloat16(0.125)


def dot2(a, b):
    return dot(a[0], b[0]) + dot(a[1], b[1])


def halves(product, a, *rest):
    middle = a[0].shape[0] // 2
    parts = [tuple(x[rows] for x in a) for rows in (slice(0, middle), slice(middle, None))]
    return jnp.concatenate([product(part, *rest) for part in parts], axis=0)


def eye(size):
    shape = (size, size)
    return lax.broadcasted_iota(jnp.int32, shape, 0) == lax.broadcasted_iota(jnp.int32, shape, 1)


def call(kernel, out_shape, in_specs, scratch_shapes=(), vmem=8, flops=0):
    count = len(out_shape) if isinstance(out_shape, tuple) else 0
    return pl.pallas_call(
        kernel,
        out_shape=out_shape,
        in_specs=in_specs,
        out_specs=(VMEM,) * count if count else VMEM,
        scratch_shapes=scratch_shapes,
        compiler_params=pltpu.CompilerParams(vmem_limit_bytes=vmem << 20),
        cost_estimate=pl.CostEstimate(flops=flops, bytes_accessed=1 << 18, transcendentals=0),
    )


def position():
    me = lax.axis_index("energy") * lax.axis_size("tile") + lax.axis_index("tile")
    return me, me + 1 - 2 * lax.rem(me, 2)


def energy_of(k, half):
    me, _ = position()
    return 2 * lax.rem(me // 2 + jnp.minimum(k, half - 1), half) + lax.rem(me, 2)


def weighted(h_ref, rows, columns, scales, targets):
    diagonal = eye(h_ref.shape[0])

    def one(row, column, factors):
        n = h_ref[...] * (SHARE / row[:1])
        first = split(n)
        square = dot3(first, first) * (1.0 / SHARE)
        yield
        first, second = blend(n), blend(square)
        cube = dot2(second, first)
        fourth = dot2(second, second)
        yield
        head = n + square + cube
        rest = dot2(blend(fourth), blend(head))
        yield
        s = head + fourth + rest
        root = jnp.where(diagonal, SHARE + s, s) * column
        high, low = split(root * (jnp.sqrt(row[1:]) / SHARE))
        flip = ((1,), (1,))
        part = dot(high, high * jnp.bfloat16(0.5), flip) + dot(high, low, flip)
        yield
        for factor, target in zip(factors, targets):
            target[...] += factor * part

    waiting = [one(row, columns[u], scales[u]) for u, row in enumerate(rows)]
    running = []
    while waiting or running:
        running += waiting[:1]
        waiting = waiting[1:]
        for stages in list(running):
            if next(stages, 0) == 0:
                running.remove(stages)


def own_kernel(
    listed_t, coupling, kernel_ref, h_ref, row_ref,
    weight_ref, lanes_ref, scales_ref, mine_ref, other_ref,
):
    tiles, listed = coupling.shape
    norb = weight_ref.shape[0]
    b = norb // tiles
    row = row_ref[...]
    column = jnp.broadcast_to(1.0 / row[:1], (8, norb)).T[:, :1]
    me, partner = position()
    mine_ref[...] = jnp.zeros_like(mine_ref)
    other_ref[...] = jnp.zeros_like(other_ref)
    scales = [kernel_ref[target, me] for target in (me, partner)]
    weighted(h_ref, [row], [column], [scales], (mine_ref, other_ref))
    half = kernel_ref.shape[0] // 2
    for i, target in enumerate((me, partner)):
        for k in range(1, scales_ref.shape[1]):
            scale = kernel_ref[target, energy_of(k, half)] if k < half else 0.0
            scales_ref[i, k] = jnp.full((1, LANES), scale, f32)
    group = lax.broadcasted_iota(jnp.int32, (b, norb), 1) // b
    slot = lax.broadcasted_iota(jnp.int32, (1, LANES), 1) // b
    for t in range(tiles):
        weight = jnp.where(group == t, coupling[t, 0], 0.0)
        tile = jnp.full((1, LANES), t, jnp.int32)
        for j in range(1, listed):
            m = listed_t[j - 1, t]
            weight = jnp.where(group == m, coupling[t, j], weight)
            tile = jnp.where(slot == j, m, tile)
        weight_ref[pl.ds(t * b, b), :] = weight
        lanes_ref[pl.ds(t, 1), :LANES] = tile
        lanes_ref[pl.ds(t, 1), LANES:] = jnp.full((1, LANES), listed_t[listed - 2, t], jnp.int32)


def first_kernel(
    scales_ref, levels_ref, h_ref, own_mine_ref, own_other_ref, mine_ref, other_ref, columns
):
    norb = h_ref.shape[0]
    half = levels_ref.shape[0] // 2
    groups = columns.shape[0]
    unroll = (scales_ref.shape[1] - 1) // groups
    for g in range(groups):
        rows = [levels_ref[energy_of(1 + g * unroll + u, half), :1] for u in range(unroll)]
        rows += rows[:1] * (-unroll % 8)
        columns[g, :, : len(rows)] = (1.0 / jnp.concatenate(rows, axis=0)).T
    mine_ref[...] = own_mine_ref[...]
    other_ref[...] = own_other_ref[...]

    def group(g, carry):
        ks = [1 + g * unroll + u for u in range(unroll)]
        rows = [levels_ref[energy_of(k, half)] for k in ks]
        scales = [
            [jnp.concatenate([scales_ref[i, k]] * (norb // LANES), axis=1) for i in range(2)]
            for k in ks
        ]
        weighted(
            h_ref, rows, [columns[g, :, u : u + 1] for u in range(unroll)], scales,
            (mine_ref, other_ref),
        )
        return carry

    lax.fori_loop(0, groups, group, 0)


def lesser_function(weight_ref, mine_ref, other_ref, h_ref, row_ref):
    norb = h_ref.shape[0]
    total = mine_ref[...] + other_ref[...]
    sigma = (total + total.T) * weight_ref[...]
    diagonal = eye(norb)
    row = row_ref[...]
    inverse_row = 1.0 / row[:1]
    inverse_column = jnp.broadcast_to(inverse_row, (8, norb)).T[:, :1]
    n = (h_ref[...] + sigma) * (SHARE * inverse_row)
    first = split(n)
    square = halves(dot3, first, first) * (1.0 / SHARE)
    first, second = blend(n), blend(square)
    cube = dot2(second, first)
    fourth = dot2(second, second)
    head = n + square + cube
    s = head + fourth + halves(dot2, blend(fourth), blend(head))
    green = split(jnp.where(diagonal, SHARE + s, s) * (inverse_column / SHARE))
    source = jnp.where(diagonal, sigma + row[1:], sigma)
    left = halves(dot3, green, split(source))
    lesser = halves(dot3, split(left), green, ((1,), (1,)))
    return lesser, jnp.sum(jnp.where(diagonal, lesser, 0.0), axis=0, keepdims=True)


def second_kernel(
    lanes_ref, weight_ref, mine_ref, other_ref, h_ref, row_ref,
    out_ref, density_ref, lesser_ref,
):
    lesser, density_ref[...] = lesser_function(
        weight_ref, mine_ref, other_ref, h_ref, row_ref
    )
    lesser_ref[...] = lesser
    norb = lesser_ref.shape[0]
    tiles = lanes_ref.shape[0]
    b = norb // tiles
    per = LANES // b
    shape = (per, LANES)
    lane = lax.broadcasted_iota(jnp.int32, shape, 1)
    own = lane // b == lax.broadcasted_iota(jnp.int32, shape, 0)

    def take(rows, tile):
        index = lax.rem(tile, per) * b + lax.rem(lane, b)
        value = None
        for h in range(norb // LANES):
            part = jnp.take_along_axis(
                lesser_ref[rows, pl.ds(h * LANES, LANES)], index, axis=1, mode="promise_in_bounds"
            )
            value = part if value is None else jnp.where(tile // per == h, part, value)
        return value

    for t in range(tiles):
        tile = jnp.broadcast_to(lanes_ref[pl.ds(t, 1), :LANES], shape)
        last = jnp.broadcast_to(lanes_ref[pl.ds(t, 1), LANES:], shape)
        for part in range(b // per):
            rows = pl.ds(t * b + part * per, per)
            first = (t * (b // per) + part) * (per + 1)
            out_ref[pl.ds(first, per), :] = take(rows, tile)
            out_ref[pl.ds(first + per, 1), :] = jnp.sum(
                jnp.where(own, take(rows, last), 0.0), axis=0, keepdims=True
            )


def mix_kernel(kernel_ref, in_ref, out_ref):
    count = kernel_ref.shape[0]
    stride = in_ref.shape[0] // count
    kernel = split(kernel_ref[...])
    parts = [
        dot3(kernel, split(in_ref[pl.ds(k, count, stride=stride), :])) for k in range(stride)
    ]
    per = stride - 1
    width = LANES // per
    group = lax.broadcasted_iota(jnp.int32, (count, LANES), 1) // width
    step = 1
    while step < per:
        upper = (group // step) % 2 == 1
        for k in range(per):
            if k // step % 2 == 0:
                low, high = parts[k], parts[k + step]
                parts[k] = jnp.where(upper, pltpu.roll(high, step * width, 1), low)
                parts[k + step] = jnp.where(upper, high, pltpu.roll(low, LANES - step * width, 1))
        step *= 2
    for k in range(stride):
        out_ref[pl.ds(k, count, stride=stride), :] = parts[k]


def last_kernel(coupling_ref, in_ref, diagonal_ref, out_ref, density_ref):
    density_ref[...] = diagonal_ref[...]
    listed, tiles, size = out_ref.shape
    parts = size // LANES
    for j in range(listed):
        weight = coupling_ref[:, j : j + 1]
        for part in range(parts):
            rows = in_ref[pl.ds(part * listed + j, tiles, stride=parts * listed), :]
            out_ref[j, :, pl.ds(part * LANES, LANES)] = rows * weight


def row_kernel(
    listed_t, weight_ref, mine_ref, other_ref, h_ref, row_ref,
    out_ref, density_ref, lesser_ref, flat,
):
    lesser, density_ref[...] = lesser_function(
        weight_ref, mine_ref, other_ref, h_ref, row_ref
    )
    lesser_ref[...] = lesser
    norb = lesser_ref.shape[0]
    listed = listed_t.shape[0] + 1
    tiles = listed_t.shape[1]
    b = norb // tiles
    flatten(lesser_ref, flat, b)
    per = out_ref.shape[2] // LANES
    parts = b * b // LANES
    for t in range(tiles):
        for j in range(listed):
            m = t if j == 0 else listed_t[j - 1, t]
            for part in range(parts):
                r = (t * listed + j) * parts + part
                out_ref[r // per, :, pl.ds(r % per * LANES, LANES)] = flat[part, t * tiles + m]


def flatten(src, dst, b):
    per = LANES // b
    shape = (per, LANES)
    lane = lax.broadcasted_iota(jnp.int32, shape, 1)
    index = lax.broadcasted_iota(jnp.int32, shape, 0) * b + lax.rem(lane, b)
    norb = src.shape[0]
    for t in range(norb // b):
        for q in range(b // per):
            for h in range(norb // LANES):
                value = None
                for a in range(per):
                    row = src[pl.ds(t * b + q * per + a, 1), pl.ds(h * LANES, LANES)]
                    moved = jnp.take_along_axis(
                        jnp.broadcast_to(row, shape), index, axis=1, mode="promise_in_bounds"
                    )
                    value = moved if value is None else jnp.where(lane // b == a, moved, value)
                dst[q, pl.ds(t * b + h * per, per), 0, :] = value


def row_mix_kernel(kernel_ref, in_ref, out_ref):
    count = in_ref.shape[0]
    kernel = split(kernel_ref[...])
    for k in range(in_ref.shape[2] // LANES):
        part = pl.ds(k * LANES, LANES)
        mixed = dot3(kernel, split(in_ref[:, :, part].reshape(count, LANES)))
        out_ref[:, :, part] = mixed.reshape(count, 1, LANES)


def row_last_kernel(coupling, in_ref, diagonal_ref, out_ref, density_ref):
    density_ref[...] = diagonal_ref[...]
    listed, tiles, size = out_ref.shape
    per = in_ref.shape[2] // LANES
    for t in range(tiles):
        for j in range(listed):
            for part in range(size // LANES):
                r = (t * listed + j) * (size // LANES) + part
                row = in_ref[r // per, :, pl.ds(r % per * LANES, LANES)]
                out_ref[j, pl.ds(t, 1), pl.ds(part * LANES, LANES)] = row * coupling[t, j]


def local(hamiltonian, onsite, inject, phonon_kernel, coupling, neighbours):
    axes = ("energy", "tile")
    tile_count = lax.axis_size("tile")
    count = lax.axis_size("energy") * tile_count
    norb = hamiltonian.shape[0]
    tiles, listed = coupling.shape
    b = norb // tiles
    listed_t = neighbours.T

    def array(*shape, dtype=f32):
        return jax.ShapeDtypeStruct(shape, dtype)

    def exchange(x):
        return lax.all_to_all(x, axes, split_axis=0, concat_axis=0, tiled=True)

    row = jnp.stack([onsite, inject], axis=1).reshape(2, norb)
    all_levels = exchange(jnp.broadcast_to(row[None], (count, 2, norb)))
    half = count // 2
    groups = -(-(half - 1) // UNROLL)
    energy_flops = 14 * 2 * norb**3
    dense = array(norb, norb)
    scales = array(2, 1 + groups * UNROLL, 1, LANES)
    lanes = array(tiles, 2 * LANES, dtype=jnp.int32)
    weight, lanes, scales, mine, other = call(
        own_kernel,
        (dense, lanes, scales, dense, dense),
        [SMEM] * 3 + [VMEM] * 2,
        flops=energy_flops,
    )(listed_t, coupling, phonon_kernel, hamiltonian, row)
    mine, other = call(
        first_kernel,
        (dense, dense),
        [VMEM] * 5,
        [pltpu.VMEM((groups, norb, LANES), f32)],
        vmem=24,
        flops=(half - 1) * energy_flops,
    )(scales, all_levels, hamiltonian, mine, other)
    other = lax.ppermute(other, "tile", [(i, i + 1 - 2 * (i % 2)) for i in range(tile_count)])

    operands = (weight, mine, other, hamiltonian, row)
    green_flops = 18 * 2 * norb**3
    scratch = pltpu.VMEM((norb, norb), f32)
    results = (array(listed, tiles, b * b), array(1, norb))
    if count * LANES == norb * b and listed * b == LANES + b:
        rows = array(norb * listed * b // LANES, LANES)
        pieces, density = call(
            second_kernel,
            (rows, array(1, norb)),
            [VMEM] * 6,
            [scratch],
            flops=green_flops,
        )(lanes, *operands)
        flat = (count, 1, rows.shape[0] * LANES // count)
        pieces = exchange(pieces.reshape(flat)).reshape(rows.shape)
        pieces = call(mix_kernel, rows, [VMEM] * 2)(phonon_kernel, pieces)
        pieces = exchange(pieces.reshape(flat)).reshape(rows.shape)
        blocks, density = call(last_kernel, results, [VMEM] * 3)(coupling, pieces, density)
    else:
        per = -(-norb * listed * b // (LANES * count))
        rows = array(count, 1, per * LANES)
        pieces, density = call(
            row_kernel,
            (rows, array(1, norb)),
            [SMEM] + [VMEM] * 5,
            [scratch, pltpu.VMEM((norb // LANES, norb, 1, LANES), f32)],
            flops=green_flops,
        )(listed_t, *operands)
        pieces = call(row_mix_kernel, rows, [VMEM] * 2)(phonon_kernel, exchange(pieces))
        blocks, density = call(row_last_kernel, results, [SMEM, VMEM, VMEM])(
            coupling, exchange(pieces), density
        )
    return blocks.transpose(1, 0, 2)[None], density


def solution(mesh):
    in_specs = (P(), P(("energy", "tile"), None), P(("energy", "tile"), None), P(), P(), P())
    out_specs = (P(("energy", "tile"), None, None, None), P(("energy", "tile"), None))
    return jax.shard_map(local, mesh=mesh, in_specs=in_specs, out_specs=out_specs, check_vma=False)
```

```python
import jax
import jax.numpy as jnp
from jax import lax
from jax.experimental import pallas as pl
from jax.experimental.pallas import tpu as pltpu
from jax.sharding import PartitionSpec as P

LANES = 128
UNROLL = 15

f32 = jnp.float32
VMEM = pl.BlockSpec(memory_space=pltpu.VMEM)
SMEM = pl.BlockSpec(memory_space=pltpu.SMEM)


def split(x):
    high = x.astype(jnp.bfloat16)
    return high, (x - high.astype(f32)).astype(jnp.bfloat16)


def dot(a, b, dims=((1,), (0,))):
    return lax.dot_general(a, b, (dims, ((), ())), preferred_element_type=f32)


def dot3(a, b, dims=((1,), (0,))):
    return dot(a[0], b[0], dims) + (dot(a[0], b[1], dims) + dot(a[1], b[0], dims))


SHARE = 64.0 / 65.0


def blend(x):
    high = x.astype(jnp.bfloat16)
    low = (x - high.astype(f32)).astype(jnp.bfloat16)
    return high, low * jnp.bfloat16(8.125) + high * jnp.bfloat16(0.125)


def dot2(a, b):
    return dot(a[0], b[0]) + dot(a[1], b[1])


def halves(product, a, *rest):
    middle = a[0].shape[0] // 2
    parts = [tuple(x[rows] for x in a) for rows in (slice(0, middle), slice(middle, None))]
    return jnp.concatenate([product(part, *rest) for part in parts], axis=0)


def eye(size):
    shape = (size, size)
    return lax.broadcasted_iota(jnp.int32, shape, 0) == lax.broadcasted_iota(jnp.int32, shape, 1)


def call(kernel, out_shape, in_specs, scratch_shapes=(), vmem=8, flops=0):
    count = len(out_shape) if isinstance(out_shape, tuple) else 0
    return pl.pallas_call(
        kernel,
        out_shape=out_shape,
        in_specs=in_specs,
        out_specs=(VMEM,) * count if count else VMEM,
        scratch_shapes=scratch_shapes,
        compiler_params=pltpu.CompilerParams(vmem_limit_bytes=vmem << 20),
        cost_estimate=pl.CostEstimate(flops=flops, bytes_accessed=1 << 18, transcendentals=0),
    )


def position():
    me = lax.axis_index("energy") * lax.axis_size("tile") + lax.axis_index("tile")
    return me, me + 1 - 2 * lax.rem(me, 2)


def energy_of(k, half):
    me, _ = position()
    return 2 * lax.rem(me // 2 + jnp.minimum(k, half - 1), half) + lax.rem(me, 2)


def weighted(h_ref, rows, columns, scales, targets):
    diagonal = eye(h_ref.shape[0])

    def one(row, column, factors):
        n = h_ref[...] * (SHARE / row[:1])
        first = split(n)
        square = dot3(first, first) * (1.0 / SHARE)
        yield
        first, second = blend(n), blend(square)
        cube = dot2(second, first)
        fourth = dot2(second, second)
        yield
        head = n + square + cube
        rest = dot2(blend(fourth), blend(head))
        yield
        s = head + fourth + rest
        root = jnp.where(diagonal, SHARE + s, s) * column
        high, low = split(root * (jnp.sqrt(row[1:]) / SHARE))
        flip = ((1,), (1,))
        part = dot(high, high * jnp.bfloat16(0.5), flip) + dot(high, low, flip)
        yield
        for factor, target in zip(factors, targets):
            target[...] += factor * part

    waiting = [one(row, columns[u], scales[u]) for u, row in enumerate(rows)]
    running = []
    while waiting or running:
        running += waiting[:1]
        waiting = waiting[1:]
        for stages in list(running):
            if next(stages, 0) == 0:
                running.remove(stages)


def own_kernel(
    listed_t, coupling, kernel_ref, h_ref, row_ref,
    weight_ref, lanes_ref, scales_ref, mine_ref, other_ref,
):
    tiles, listed = coupling.shape
    norb = weight_ref.shape[0]
    b = norb // tiles
    row = row_ref[...]
    column = jnp.broadcast_to(1.0 / row[:1], (8, norb)).T[:, :1]
    me, partner = position()
    mine_ref[...] = jnp.zeros_like(mine_ref)
    other_ref[...] = jnp.zeros_like(other_ref)
    scales = [kernel_ref[target, me] for target in (me, partner)]
    weighted(h_ref, [row], [column], [scales], (mine_ref, other_ref))
    half = kernel_ref.shape[0] // 2
    for i, target in enumerate((me, partner)):
        for k in range(1, scales_ref.shape[1]):
            scale = kernel_ref[target, energy_of(k, half)] if k < half else 0.0
            scales_ref[i, k] = jnp.full((1, LANES), scale, f32)
    group = lax.broadcasted_iota(jnp.int32, (b, norb), 1) // b
    slot = lax.broadcasted_iota(jnp.int32, (1, LANES), 1) // b
    for t in range(tiles):
        weight = jnp.where(group == t, coupling[t, 0], 0.0)
        tile = jnp.full((1, LANES), t, jnp.int32)
        for j in range(1, listed):
            m = listed_t[j - 1, t]
            weight = jnp.where(group == m, coupling[t, j], weight)
            tile = jnp.where(slot == j, m, tile)
        weight_ref[pl.ds(t * b, b), :] = weight
        lanes_ref[pl.ds(t, 1), :LANES] = tile
        lanes_ref[pl.ds(t, 1), LANES:] = jnp.full((1, LANES), listed_t[listed - 2, t], jnp.int32)


def first_kernel(
    scales_ref, levels_ref, h_ref, own_mine_ref, own_other_ref, mine_ref, other_ref, columns
):
    norb = h_ref.shape[0]
    half = levels_ref.shape[0] // 2
    groups = columns.shape[0]
    unroll = (scales_ref.shape[1] - 1) // groups
    for g in range(groups):
        rows = [levels_ref[energy_of(1 + g * unroll + u, half), :1] for u in range(unroll)]
        rows += rows[:1] * (-unroll % 8)
        columns[g, :, : len(rows)] = (1.0 / jnp.concatenate(rows, axis=0)).T
    mine_ref[...] = own_mine_ref[...]
    other_ref[...] = own_other_ref[...]

    def group(g, carry):
        ks = [1 + g * unroll + u for u in range(unroll)]
        rows = [levels_ref[energy_of(k, half)] for k in ks]
        scales = [
            [jnp.concatenate([scales_ref[i, k]] * (norb // LANES), axis=1) for i in range(2)]
            for k in ks
        ]
        weighted(
            h_ref, rows, [columns[g, :, u : u + 1] for u in range(unroll)], scales,
            (mine_ref, other_ref),
        )
        return carry

    lax.fori_loop(0, groups, group, 0)


def lesser_function(weight_ref, mine_ref, other_ref, h_ref, row_ref):
    norb = h_ref.shape[0]
    total = mine_ref[...] + other_ref[...]
    sigma = (total + total.T) * weight_ref[...]
    diagonal = eye(norb)
    row = row_ref[...]
    inverse_row = 1.0 / row[:1]
    inverse_column = jnp.broadcast_to(inverse_row, (8, norb)).T[:, :1]
    n = (h_ref[...] + sigma) * inverse_row
    first = split(n)
    square = halves(dot3, first, first)
    second = split(square)
    cube = dot3(second, first)
    fourth = dot3(second, second)
    head = n + square + cube
    s = head + fourth + halves(dot3, split(fourth), split(head))
    green = split(jnp.where(diagonal, 1.0 + s, s) * inverse_column)
    source = jnp.where(diagonal, sigma + row[1:], sigma)
    left = halves(dot3, green, split(source))
    lesser = halves(dot3, split(left), green, ((1,), (1,)))
    return lesser, jnp.sum(jnp.where(diagonal, lesser, 0.0), axis=0, keepdims=True)


def second_kernel(
    lanes_ref, weight_ref, mine_ref, other_ref, h_ref, row_ref,
    out_ref, density_ref, lesser_ref,
):
    lesser, density_ref[...] = lesser_function(
        weight_ref, mine_ref, other_ref, h_ref, row_ref
    )
    lesser_ref[...] = lesser
    norb = lesser_ref.shape[0]
    tiles = lanes_ref.shape[0]
    b = norb // tiles
    per = LANES // b
    shape = (per, LANES)
    lane = lax.broadcasted_iota(jnp.int32, shape, 1)
    own = lane // b == lax.broadcasted_iota(jnp.int32, shape, 0)

    def take(rows, tile):
        index = lax.rem(tile, per) * b + lax.rem(lane, b)
        value = None
        for h in range(norb // LANES):
            part = jnp.take_along_axis(
                lesser_ref[rows, pl.ds(h * LANES, LANES)], index, axis=1, mode="promise_in_bounds"
            )
            value = part if value is None else jnp.where(tile // per == h, part, value)
        return value

    for t in range(tiles):
        tile = jnp.broadcast_to(lanes_ref[pl.ds(t, 1), :LANES], shape)
        last = jnp.broadcast_to(lanes_ref[pl.ds(t, 1), LANES:], shape)
        for part in range(b // per):
            rows = pl.ds(t * b + part * per, per)
            first = (t * (b // per) + part) * (per + 1)
            out_ref[pl.ds(first, per), :] = take(rows, tile)
            out_ref[pl.ds(first + per, 1), :] = jnp.sum(
                jnp.where(own, take(rows, last), 0.0), axis=0, keepdims=True
            )


def mix_kernel(kernel_ref, in_ref, out_ref):
    count = kernel_ref.shape[0]
    stride = in_ref.shape[0] // count
    kernel = split(kernel_ref[...])
    parts = [
        dot3(kernel, split(in_ref[pl.ds(k, count, stride=stride), :])) for k in range(stride)
    ]
    per = stride - 1
    width = LANES // per
    group = lax.broadcasted_iota(jnp.int32, (count, LANES), 1) // width
    step = 1
    while step < per:
        upper = (group // step) % 2 == 1
        for k in range(per):
            if k // step % 2 == 0:
                low, high = parts[k], parts[k + step]
                parts[k] = jnp.where(upper, pltpu.roll(high, step * width, 1), low)
                parts[k + step] = jnp.where(upper, high, pltpu.roll(low, LANES - step * width, 1))
        step *= 2
    for k in range(stride):
        out_ref[pl.ds(k, count, stride=stride), :] = parts[k]


def last_kernel(coupling_ref, in_ref, diagonal_ref, out_ref, density_ref):
    density_ref[...] = diagonal_ref[...]
    listed, tiles, size = out_ref.shape
    parts = size // LANES
    for j in range(listed):
        weight = coupling_ref[:, j : j + 1]
        for part in range(parts):
            rows = in_ref[pl.ds(part * listed + j, tiles, stride=parts * listed), :]
            out_ref[j, :, pl.ds(part * LANES, LANES)] = rows * weight


def row_kernel(
    listed_t, weight_ref, mine_ref, other_ref, h_ref, row_ref,
    out_ref, density_ref, lesser_ref, flat,
):
    lesser, density_ref[...] = lesser_function(
        weight_ref, mine_ref, other_ref, h_ref, row_ref
    )
    lesser_ref[...] = lesser
    norb = lesser_ref.shape[0]
    listed = listed_t.shape[0] + 1
    tiles = listed_t.shape[1]
    b = norb // tiles
    flatten(lesser_ref, flat, b)
    per = out_ref.shape[2] // LANES
    parts = b * b // LANES
    for t in range(tiles):
        for j in range(listed):
            m = t if j == 0 else listed_t[j - 1, t]
            for part in range(parts):
                r = (t * listed + j) * parts + part
                out_ref[r // per, :, pl.ds(r % per * LANES, LANES)] = flat[part, t * tiles + m]


def flatten(src, dst, b):
    per = LANES // b
    shape = (per, LANES)
    lane = lax.broadcasted_iota(jnp.int32, shape, 1)
    index = lax.broadcasted_iota(jnp.int32, shape, 0) * b + lax.rem(lane, b)
    norb = src.shape[0]
    for t in range(norb // b):
        for q in range(b // per):
            for h in range(norb // LANES):
                value = None
                for a in range(per):
                    row = src[pl.ds(t * b + q * per + a, 1), pl.ds(h * LANES, LANES)]
                    moved = jnp.take_along_axis(
                        jnp.broadcast_to(row, shape), index, axis=1, mode="promise_in_bounds"
                    )
                    value = moved if value is None else jnp.where(lane // b == a, moved, value)
                dst[q, pl.ds(t * b + h * per, per), 0, :] = value


def row_mix_kernel(kernel_ref, in_ref, out_ref):
    count = in_ref.shape[0]
    kernel = split(kernel_ref[...])
    for k in range(in_ref.shape[2] // LANES):
        part = pl.ds(k * LANES, LANES)
        mixed = dot3(kernel, split(in_ref[:, :, part].reshape(count, LANES)))
        out_ref[:, :, part] = mixed.reshape(count, 1, LANES)


def row_last_kernel(coupling, in_ref, diagonal_ref, out_ref, density_ref):
    density_ref[...] = diagonal_ref[...]
    listed, tiles, size = out_ref.shape
    per = in_ref.shape[2] // LANES
    for t in range(tiles):
        for j in range(listed):
            for part in range(size // LANES):
                r = (t * listed + j) * (size // LANES) + part
                row = in_ref[r // per, :, pl.ds(r % per * LANES, LANES)]
                out_ref[j, pl.ds(t, 1), pl.ds(part * LANES, LANES)] = row * coupling[t, j]


def local(hamiltonian, onsite, inject, phonon_kernel, coupling, neighbours):
    axes = ("energy", "tile")
    tile_count = lax.axis_size("tile")
    count = lax.axis_size("energy") * tile_count
    norb = hamiltonian.shape[0]
    tiles, listed = coupling.shape
    b = norb // tiles
    listed_t = neighbours.T

    def array(*shape, dtype=f32):
        return jax.ShapeDtypeStruct(shape, dtype)

    def exchange(x):
        return lax.all_to_all(x, axes, split_axis=0, concat_axis=0, tiled=True)

    row = jnp.stack([onsite, inject], axis=1).reshape(2, norb)
    all_levels = exchange(jnp.broadcast_to(row[None], (count, 2, norb)))
    half = count // 2
    groups = -(-(half - 1) // UNROLL)
    energy_flops = 14 * 2 * norb**3
    dense = array(norb, norb)
    scales = array(2, 1 + groups * UNROLL, 1, LANES)
    lanes = array(tiles, 2 * LANES, dtype=jnp.int32)
    weight, lanes, scales, mine, other = call(
        own_kernel,
        (dense, lanes, scales, dense, dense),
        [SMEM] * 3 + [VMEM] * 2,
        flops=energy_flops,
    )(listed_t, coupling, phonon_kernel, hamiltonian, row)
    mine, other = call(
        first_kernel,
        (dense, dense),
        [VMEM] * 5,
        [pltpu.VMEM((groups, norb, LANES), f32)],
        vmem=24,
        flops=(half - 1) * energy_flops,
    )(scales, all_levels, hamiltonian, mine, other)
    other = lax.ppermute(other, "tile", [(i, i + 1 - 2 * (i % 2)) for i in range(tile_count)])

    operands = (weight, mine, other, hamiltonian, row)
    green_flops = 18 * 2 * norb**3
    scratch = pltpu.VMEM((norb, norb), f32)
    results = (array(listed, tiles, b * b), array(1, norb))
    if count * LANES == norb * b and listed * b == LANES + b:
        rows = array(norb * listed * b // LANES, LANES)
        pieces, density = call(
            second_kernel,
            (rows, array(1, norb)),
            [VMEM] * 6,
            [scratch],
            flops=green_flops,
        )(lanes, *operands)
        flat = (count, 1, rows.shape[0] * LANES // count)
        pieces = exchange(pieces.reshape(flat)).reshape(rows.shape)
        pieces = call(mix_kernel, rows, [VMEM] * 2)(phonon_kernel, pieces)
        pieces = exchange(pieces.reshape(flat)).reshape(rows.shape)
        blocks, density = call(last_kernel, results, [VMEM] * 3)(coupling, pieces, density)
    else:
        per = -(-norb * listed * b // (LANES * count))
        rows = array(count, 1, per * LANES)
        pieces, density = call(
            row_kernel,
            (rows, array(1, norb)),
            [SMEM] + [VMEM] * 5,
            [scratch, pltpu.VMEM((norb // LANES, norb, 1, LANES), f32)],
            flops=green_flops,
        )(listed_t, *operands)
        pieces = call(row_mix_kernel, rows, [VMEM] * 2)(phonon_kernel, exchange(pieces))
        blocks, density = call(row_last_kernel, results, [SMEM, VMEM, VMEM])(
            coupling, exchange(pieces), density
        )
    return blocks.transpose(1, 0, 2)[None], density


def solution(mesh):
    in_specs = (P(), P(("energy", "tile"), None), P(("energy", "tile"), None), P(), P(), P())
    out_specs = (P(("energy", "tile"), None, None, None), P(("energy", "tile"), None))
    return jax.shard_map(local, mesh=mesh, in_specs=in_specs, out_specs=out_specs, check_vma=False)
```

```python
import jax
import jax.numpy as jnp
from jax import lax
from jax.experimental import pallas as pl
from jax.experimental.pallas import tpu as pltpu
from jax.sharding import PartitionSpec as P

LANES = 128
UNROLL = 15

f32 = jnp.float32
VMEM = pl.BlockSpec(memory_space=pltpu.VMEM)
SMEM = pl.BlockSpec(memory_space=pltpu.SMEM)


def split(x):
    high = x.astype(jnp.bfloat16)
    return high, (x - high.astype(f32)).astype(jnp.bfloat16)


def dot(a, b, dims=((1,), (0,))):
    return lax.dot_general(a, b, (dims, ((), ())), preferred_element_type=f32)


def dot3(a, b, dims=((1,), (0,))):
    return dot(a[0], b[0], dims) + (dot(a[0], b[1], dims) + dot(a[1], b[0], dims))


SHARE = 64.0 / 65.0


def blend(x):
    high = x.astype(jnp.bfloat16)
    low = (x - high.astype(f32)).astype(jnp.bfloat16)
    return high, low * jnp.bfloat16(8.125) + high * jnp.bfloat16(0.125)


def dot2(a, b):
    return dot(a[0], b[0]) + dot(a[1], b[1])


def halves(product, a, *rest):
    middle = a[0].shape[0] // 2
    parts = [tuple(x[rows] for x in a) for rows in (slice(0, middle), slice(middle, None))]
    return jnp.concatenate([product(part, *rest) for part in parts], axis=0)


def eye(size):
    shape = (size, size)
    return lax.broadcasted_iota(jnp.int32, shape, 0) == lax.broadcasted_iota(jnp.int32, shape, 1)


def call(kernel, out_shape, in_specs, scratch_shapes=(), vmem=8, flops=0):
    count = len(out_shape) if isinstance(out_shape, tuple) else 0
    return pl.pallas_call(
        kernel,
        out_shape=out_shape,
        in_specs=in_specs,
        out_specs=(VMEM,) * count if count else VMEM,
        scratch_shapes=scratch_shapes,
        compiler_params=pltpu.CompilerParams(vmem_limit_bytes=vmem << 20),
        cost_estimate=pl.CostEstimate(flops=flops, bytes_accessed=1 << 18, transcendentals=0),
    )


def position():
    me = lax.axis_index("energy") * lax.axis_size("tile") + lax.axis_index("tile")
    return me, me + 1 - 2 * lax.rem(me, 2)


def energy_of(k, half):
    me, _ = position()
    return 2 * lax.rem(me // 2 + jnp.minimum(k, half - 1), half) + lax.rem(me, 2)


def column(row):
    return jnp.broadcast_to(row, (8, row.shape[1])).T[:, :1]


def weighted(h_ref, rows, scales, bases, targets):
    diagonal = eye(h_ref.shape[0])

    def one(row, factors, bases):
        n = h_ref[...] * (SHARE / row[:1])
        first = split(n)
        square = dot3(first, first) * (1.0 / SHARE)
        yield
        first, second = blend(n), blend(square)
        cube = dot2(second, first)
        fourth = dot2(second, second)
        yield
        head = n + square + cube
        rest = dot2(blend(fourth), blend(head))
        yield
        s = head + fourth + rest
        root = jnp.where(diagonal, SHARE + s, s) * column(1.0 / row[:1])
        high, low = split(root * (jnp.sqrt(row[1:]) / SHARE))
        flip = ((1,), (1,))
        part = dot(high, high * jnp.bfloat16(0.5), flip) + dot(high, low, flip)
        yield
        for factor, base, target in zip(factors, bases, targets):
            target[...] = base[...] + factor * part

    waiting = [one(row, scales[u], targets if u else bases) for u, row in enumerate(rows)]
    running = []
    while waiting or running:
        running += waiting[:1]
        waiting = waiting[1:]
        for stages in list(running):
            if next(stages, 0) == 0:
                running.remove(stages)


def own_kernel(
    listed_t, coupling, kernel_ref, h_ref, row_ref,
    weight_ref, lanes_ref, scales_ref, mine_ref, other_ref,
):
    tiles, listed = coupling.shape
    norb = weight_ref.shape[0]
    b = norb // tiles
    row = row_ref[...]
    me, partner = position()
    mine_ref[...] = jnp.zeros_like(mine_ref)
    other_ref[...] = jnp.zeros_like(other_ref)
    scales = [kernel_ref[target, me] for target in (me, partner)]
    targets = (mine_ref, other_ref)
    weighted(h_ref, [row], [scales], targets, targets)
    half = kernel_ref.shape[0] // 2
    for i, target in enumerate((me, partner)):
        for k in range(1, scales_ref.shape[1]):
            scale = kernel_ref[target, energy_of(k, half)] if k < half else 0.0
            scales_ref[i, k] = jnp.full((1, LANES), scale, f32)
    group = lax.broadcasted_iota(jnp.int32, (b, norb), 1) // b
    slot = lax.broadcasted_iota(jnp.int32, (1, LANES), 1) // b
    for t in range(tiles):
        weight = jnp.where(group == t, coupling[t, 0], 0.0)
        tile = jnp.full((1, LANES), t, jnp.int32)
        for j in range(1, listed):
            m = listed_t[j - 1, t]
            weight = jnp.where(group == m, coupling[t, j], weight)
            tile = jnp.where(slot == j, m, tile)
        weight_ref[pl.ds(t * b, b), :] = weight
        lanes_ref[pl.ds(t, 1), :LANES] = tile
        lanes_ref[pl.ds(t, 1), LANES:] = jnp.full((1, LANES), listed_t[listed - 2, t], jnp.int32)


def first_kernel(
    scales_ref, levels_ref, h_ref, own_mine_ref, own_other_ref, mine_ref, other_ref
):
    norb = h_ref.shape[0]
    half = levels_ref.shape[0] // 2
    groups = -(-(half - 1) // UNROLL)
    unroll = (scales_ref.shape[1] - 1) // groups
    bases, targets = (own_mine_ref, own_other_ref), (mine_ref, other_ref)
    if groups > 1:
        mine_ref[...] = own_mine_ref[...]
        other_ref[...] = own_other_ref[...]
        bases = targets

    def group(g, carry):
        ks = [1 + g * unroll + u for u in range(unroll)]
        rows = [levels_ref[energy_of(k, half)] for k in ks]
        scales = [
            [jnp.concatenate([scales_ref[i, k]] * (norb // LANES), axis=1) for i in range(2)]
            for k in ks
        ]
        weighted(h_ref, rows, scales, bases, targets)
        return carry

    lax.fori_loop(0, groups, group, 0)


def lesser_function(weight_ref, mine_ref, other_ref, h_ref, row_ref):
    norb = h_ref.shape[0]
    total = mine_ref[...] + other_ref[...]
    sigma = (total + total.T) * weight_ref[...]
    diagonal = eye(norb)
    row = row_ref[...]
    inverse_row = 1.0 / row[:1]
    inverse_column = column(inverse_row)
    n = (h_ref[...] + sigma) * inverse_row
    first = split(n)
    square = halves(dot3, first, first)
    second = split(square)
    cube = dot3(second, first)
    fourth = dot3(second, second)
    head = n + square + cube
    s = head + fourth + halves(dot3, split(fourth), split(head))
    green = split(jnp.where(diagonal, 1.0 + s, s) * inverse_column)
    source = jnp.where(diagonal, sigma + row[1:], sigma)
    left = halves(dot3, green, split(source))
    lesser = halves(dot3, split(left), green, ((1,), (1,)))
    return lesser, jnp.sum(jnp.where(diagonal, lesser, 0.0), axis=0, keepdims=True)


def second_kernel(
    lanes_ref, weight_ref, mine_ref, other_ref, h_ref, row_ref,
    out_ref, density_ref, lesser_ref,
):
    lesser, density_ref[...] = lesser_function(
        weight_ref, mine_ref, other_ref, h_ref, row_ref
    )
    lesser_ref[...] = lesser
    norb = lesser_ref.shape[0]
    tiles = lanes_ref.shape[0]
    b = norb // tiles
    per = LANES // b
    shape = (per, LANES)
    lane = lax.broadcasted_iota(jnp.int32, shape, 1)
    own = lane // b == lax.broadcasted_iota(jnp.int32, shape, 0)

    def take(rows, tile):
        index = lax.rem(tile, per) * b + lax.rem(lane, b)
        value = None
        for h in range(norb // LANES):
            part = jnp.take_along_axis(
                lesser_ref[rows, pl.ds(h * LANES, LANES)], index, axis=1, mode="promise_in_bounds"
            )
            value = part if value is None else jnp.where(tile // per == h, part, value)
        return value

    for t in range(tiles):
        tile = jnp.broadcast_to(lanes_ref[pl.ds(t, 1), :LANES], shape)
        last = jnp.broadcast_to(lanes_ref[pl.ds(t, 1), LANES:], shape)
        for part in range(b // per):
            rows = pl.ds(t * b + part * per, per)
            first = (t * (b // per) + part) * (per + 1)
            out_ref[pl.ds(first, per), :] = take(rows, tile)
            out_ref[pl.ds(first + per, 1), :] = jnp.sum(
                jnp.where(own, take(rows, last), 0.0), axis=0, keepdims=True
            )


def mix_kernel(kernel_ref, in_ref, out_ref):
    count = kernel_ref.shape[0]
    stride = in_ref.shape[0] // count
    kernel = split(kernel_ref[...])
    parts = [
        dot3(kernel, split(in_ref[pl.ds(k, count, stride=stride), :])) for k in range(stride)
    ]
    per = stride - 1
    width = LANES // per
    group = lax.broadcasted_iota(jnp.int32, (count, LANES), 1) // width
    step = 1
    while step < per:
        upper = (group // step) % 2 == 1
        for k in range(per):
            if k // step % 2 == 0:
                low, high = parts[k], parts[k + step]
                parts[k] = jnp.where(upper, pltpu.roll(high, step * width, 1), low)
                parts[k + step] = jnp.where(upper, high, pltpu.roll(low, LANES - step * width, 1))
        step *= 2
    for k in range(stride):
        out_ref[pl.ds(k, count, stride=stride), :] = parts[k]


def last_kernel(coupling_ref, in_ref, diagonal_ref, out_ref, density_ref):
    density_ref[...] = diagonal_ref[...]
    listed, tiles, size = out_ref.shape
    parts = size // LANES
    for j in range(listed):
        weight = coupling_ref[:, j : j + 1]
        for part in range(parts):
            rows = in_ref[pl.ds(part * listed + j, tiles, stride=parts * listed), :]
            out_ref[j, :, pl.ds(part * LANES, LANES)] = rows * weight


def row_kernel(
    listed_t, weight_ref, mine_ref, other_ref, h_ref, row_ref,
    out_ref, density_ref, lesser_ref, flat,
):
    lesser, density_ref[...] = lesser_function(
        weight_ref, mine_ref, other_ref, h_ref, row_ref
    )
    lesser_ref[...] = lesser
    norb = lesser_ref.shape[0]
    listed = listed_t.shape[0] + 1
    tiles = listed_t.shape[1]
    b = norb // tiles
    flatten(lesser_ref, flat, b)
    per = out_ref.shape[2] // LANES
    parts = b * b // LANES
    for t in range(tiles):
        for j in range(listed):
            m = t if j == 0 else listed_t[j - 1, t]
            for part in range(parts):
                r = (t * listed + j) * parts + part
                out_ref[r // per, :, pl.ds(r % per * LANES, LANES)] = flat[part, t * tiles + m]


def flatten(src, dst, b):
    per = LANES // b
    shape = (per, LANES)
    lane = lax.broadcasted_iota(jnp.int32, shape, 1)
    index = lax.broadcasted_iota(jnp.int32, shape, 0) * b + lax.rem(lane, b)
    norb = src.shape[0]
    for t in range(norb // b):
        for q in range(b // per):
            for h in range(norb // LANES):
                value = None
                for a in range(per):
                    row = src[pl.ds(t * b + q * per + a, 1), pl.ds(h * LANES, LANES)]
                    moved = jnp.take_along_axis(
                        jnp.broadcast_to(row, shape), index, axis=1, mode="promise_in_bounds"
                    )
                    value = moved if value is None else jnp.where(lane // b == a, moved, value)
                dst[q, pl.ds(t * b + h * per, per), 0, :] = value


def row_mix_kernel(kernel_ref, in_ref, out_ref):
    count = in_ref.shape[0]
    kernel = split(kernel_ref[...])
    for k in range(in_ref.shape[2] // LANES):
        part = pl.ds(k * LANES, LANES)
        mixed = dot3(kernel, split(in_ref[:, :, part].reshape(count, LANES)))
        out_ref[:, :, part] = mixed.reshape(count, 1, LANES)


def row_last_kernel(coupling, in_ref, diagonal_ref, out_ref, density_ref):
    density_ref[...] = diagonal_ref[...]
    listed, tiles, size = out_ref.shape
    per = in_ref.shape[2] // LANES
    for t in range(tiles):
        for j in range(listed):
            for part in range(size // LANES):
                r = (t * listed + j) * (size // LANES) + part
                row = in_ref[r // per, :, pl.ds(r % per * LANES, LANES)]
                out_ref[j, pl.ds(t, 1), pl.ds(part * LANES, LANES)] = row * coupling[t, j]


def local(hamiltonian, onsite, inject, phonon_kernel, coupling, neighbours):
    axes = ("energy", "tile")
    tile_count = lax.axis_size("tile")
    count = lax.axis_size("energy") * tile_count
    norb = hamiltonian.shape[0]
    tiles, listed = coupling.shape
    b = norb // tiles
    listed_t = neighbours.T

    def array(*shape, dtype=f32):
        return jax.ShapeDtypeStruct(shape, dtype)

    def exchange(x):
        return lax.all_to_all(x, axes, split_axis=0, concat_axis=0, tiled=True)

    row = jnp.stack([onsite, inject], axis=1).reshape(2, norb)
    all_levels = exchange(jnp.broadcast_to(row[None], (count, 2, norb)))
    half = count // 2
    groups = -(-(half - 1) // UNROLL)
    energy_flops = 14 * 2 * norb**3
    dense = array(norb, norb)
    scales = array(2, 1 + groups * UNROLL, 1, LANES)
    lanes = array(tiles, 2 * LANES, dtype=jnp.int32)
    weight, lanes, scales, mine, other = call(
        own_kernel,
        (dense, lanes, scales, dense, dense),
        [SMEM] * 3 + [VMEM] * 2,
        flops=energy_flops,
    )(listed_t, coupling, phonon_kernel, hamiltonian, row)
    mine, other = call(
        first_kernel,
        (dense, dense),
        [VMEM] * 5,
        vmem=24,
        flops=(half - 1) * energy_flops,
    )(scales, all_levels, hamiltonian, mine, other)
    other = lax.ppermute(other, "tile", [(i, i + 1 - 2 * (i % 2)) for i in range(tile_count)])

    operands = (weight, mine, other, hamiltonian, row)
    green_flops = 18 * 2 * norb**3
    scratch = pltpu.VMEM((norb, norb), f32)
    results = (array(listed, tiles, b * b), array(1, norb))
    if count * LANES == norb * b and listed * b == LANES + b:
        rows = array(norb * listed * b // LANES, LANES)
        pieces, density = call(
            second_kernel,
            (rows, array(1, norb)),
            [VMEM] * 6,
            [scratch],
            flops=green_flops,
        )(lanes, *operands)
        flat = (count, 1, rows.shape[0] * LANES // count)
        pieces = exchange(pieces.reshape(flat)).reshape(rows.shape)
        pieces = call(mix_kernel, rows, [VMEM] * 2)(phonon_kernel, pieces)
        pieces = exchange(pieces.reshape(flat)).reshape(rows.shape)
        blocks, density = call(last_kernel, results, [VMEM] * 3)(coupling, pieces, density)
    else:
        per = -(-norb * listed * b // (LANES * count))
        rows = array(count, 1, per * LANES)
        pieces, density = call(
            row_kernel,
            (rows, array(1, norb)),
            [SMEM] + [VMEM] * 5,
            [scratch, pltpu.VMEM((norb // LANES, norb, 1, LANES), f32)],
            flops=green_flops,
        )(listed_t, *operands)
        pieces = call(row_mix_kernel, rows, [VMEM] * 2)(phonon_kernel, exchange(pieces))
        blocks, density = call(row_last_kernel, results, [SMEM, VMEM, VMEM])(
            coupling, exchange(pieces), density
        )
    return blocks.transpose(1, 0, 2)[None], density


def solution(mesh):
    in_specs = (P(), P(("energy", "tile"), None), P(("energy", "tile"), None), P(), P(), P())
    out_specs = (P(("energy", "tile"), None, None, None), P(("energy", "tile"), None))
    return jax.shard_map(local, mesh=mesh, in_specs=in_specs, out_specs=out_specs, check_vma=False)
```
